512 devices in a mesh: req: 64 (over x, z), head: 8 (over y, core).
Axes of the slice: x: 4, y: 4, z: 16, core: 2. Of those that a mesh axis runs over, the one named last changes fastest.
Arguments:
- guessed_symbol_features: bfloat16 [512, 16, 2048], P('req', None, 'head'), may hold values from -6 to 6
- earlier_feature: bfloat16 [512, 2048], P('req', 'head'), may hold values from -6 to 6
- query_memory_summary: float32 [512, 16, 64, 64], P('req', 'head'), may hold values from -6 to 6
- approved_guesses: int32 [512], P('req'), may hold values from 0 to 16
- query_ordinals: int32 [512], P('req'), may hold values from 0 to 511, as said below
- restored_ordinals: int32 [64], P('req'), may hold values from 0 to 511, as said below
- symbols_following_snapshot: int32 [64], P('req'), may hold values from 1 to 32, as said below
- snapshot_summaries: float32 [64, 16, 64, 64], P('req', 'head'), may hold values from -6 to 6
- following_snapshot_features: bfloat16 [64, 32, 2048], P('req', None, 'head'), may hold values from -6 to 6
- earlier_segment_feature: bfloat16 [64, 2048], P('req', 'head'), may hold values from -6 to 6
- acceptor_coefficients: bfloat16 [2048, 1024], P(None, 'head'), may hold values from -0.125 to 0.125
- address_coefficients: bfloat16 [2048, 1024], P(None, 'head'), may hold values from -0.125 to 0.125
- payload_coefficients: bfloat16 [2048, 1024], P(None, 'head'), may hold values from -0.125 to 0.125
- lagged_interpolants: float32 [4, 2048], replicated, may hold values from 0 to 1
- fading_narrowing_matrix: bfloat16 [2048, 64], replicated, may hold values from -0.125 to 0.125
- fading_expanding_matrix: bfloat16 [64, 1024], P(None, 'head'), may hold values from -0.75 to 0.75
- lane_fading_logit: float32 [1024], P('head'), may hold values from -6 to -1
- present_step_reward: float32 [1024], P('head'), may hold values from -3 to 3
- cluster_scaling_vector: float32 [1024], P('head'), may hold values from 0.1 to 1.9
Outputs:
- verified: bfloat16 [512, 16, 1024], P('req', None, 'head')
- new_state: float32 [512, 16, 64, 64], P('req', 'head')
The draws below stay inside these ranges and needn't reach their ends.
Inputs may be any that keep to these rules, and one draw needn't show every extreme that they name: `query_ordinals`: a permutation of 0..511; request r belongs to device query_ordinals[r] // 8 of req in the balanced order. The 8 requests held on one req device belong to 8 distinct req devices in the balanced order, and each req device has 8 requests belonging to it, held on 8 distinct req devices. `restored_ordinals`: Distinct; entry j lies between (j) * 8 and (j + 1) * 8 - 1. `symbols_following_snapshot`: some entry equals 32 in every draw.
All inputs are finite; a program needn't handle non-finite values.
Results may differ from the reference program's by a relative error of at most 0.0061.
Values may be sent and summed in bfloat16 or wider, within the bound.
A program may use at most 64 MiB of HBM per device.

```python
import jax
import jax.numpy as jnp
from jax import lax

MODEL_WIDTH = 2048
HEADS = 16
PARTITION_LENGTH = 64
DECAY_RANK = 64
DRAFTS = 16
SPAN = 32
REQ_DEV = 8
LANE_COUNT = 1024
SLOTS = 1
REB_DEV = 1
REQUESTS = 512
REBUILDS = 64
N_REQ = 64


def draw_query_ordinals(key, part):
    keys_all = jax.random.split(key, 5)
    dealing = jax.random.permutation(keys_all[0], N_REQ)
    arrangement = jax.random.permutation(keys_all[1], N_REQ)
    offsets = jax.random.permutation(keys_all[2], N_REQ)[:REQ_DEV // SLOTS]
    rotate_in = jax.random.randint(keys_all[3], (N_REQ,), 0, REQ_DEV)
    rotate_out = jax.random.randint(keys_all[4], (N_REQ,), 0, REQ_DEV)
    anchors = jnp.arange(N_REQ)[:, None]
    ordinal = (jnp.arange(REQ_DEV)[None, :] + rotate_out[:, None]) % REQ_DEV
    target = dealing[(arrangement[anchors] + offsets[ordinal // SLOTS]) % N_REQ]
    placed = (ordinal + rotate_in[target]) % REQ_DEV
    return (target * REQ_DEV + placed).reshape(-1).astype(jnp.int32)


def draw_restored_ordinals(key, part):
    scores = jax.random.randint(key, (N_REQ, REQ_DEV), 0, 1 << 20) * REQ_DEV + jnp.arange(REQ_DEV)[None, :]
    chosen_summary = jnp.argsort(scores, axis=1)[:, :REB_DEV]
    return (jnp.arange(N_REQ)[:, None] * REQ_DEV + chosen_summary).reshape(-1).astype(jnp.int32)


def draw_symbols_following_snapshot(key, part):
    first_key, second_key = jax.random.split(key)
    lengths = jax.random.randint(first_key, (REBUILDS,), 1, SPAN + 1)
    marked = jax.random.randint(second_key, (), 0, REBUILDS)
    return jnp.where(jnp.arange(REBUILDS) == marked, SPAN, lengths).astype(jnp.int32)


def place_ends(drawn, key, least, largest):
    spot = [jax.random.randint(jax.random.fold_in(key, axis), (), 0, length) for axis, length in enumerate(drawn.shape)]
    longest = drawn.shape.index(max(drawn.shape))
    neighbour = spot[:longest] + [(spot[longest] + 1) % drawn.shape[longest]] + spot[longest + 1:]
    return drawn.at[tuple(spot)].set(least).at[tuple(neighbour)].set(largest)


def levels(own_key, dims, cuts, least, high):
    level = 1.0
    for dim, shards_of in cuts:
        steps = jax.random.uniform(jax.random.fold_in(jax.random.fold_in(own_key, 6), dim), (shards_of,), jnp.float32, least / len(cuts), high / len(cuts))
        level = level * jnp.repeat(jnp.exp(steps), dims[dim] // shards_of).reshape((-1,) + (1,) * (len(dims) - 1 - dim))
    return level


def gaussian(rng, shape, scale, limit, cuts=(), kind=jnp.bfloat16):
    result = scale * jax.random.normal(rng, shape, jnp.float32)
    if cuts:
        result = result * levels(rng, shape, cuts, -0.22, 0.18)
    return jnp.clip(result, -limit, limit).astype(kind)


def setup_inputs(seed: int = 0) -> dict:
    key_list = jax.random.split(jax.random.key(seed), 20)
    guessed_symbol_features = gaussian(key_list[0], (REQUESTS, DRAFTS, MODEL_WIDTH), 1.0, 6.0, ((0, 64), (2, 8)))
    earlier_feature = gaussian(key_list[1], (REQUESTS, MODEL_WIDTH), 1.0, 6.0, ((0, 64), (1, 8)))
    query_memory_summary = gaussian(key_list[2], (REQUESTS, HEADS, PARTITION_LENGTH, PARTITION_LENGTH), 1.0, 6.0, ((0, 64), (1, 8)), jnp.float32)
    approved_guesses = place_ends(jax.random.randint(key_list[3], (REQUESTS,), 0, DRAFTS + 1), jax.random.fold_in(key_list[3], 1), 0, DRAFTS).astype(jnp.int32)
    query_ordinals = draw_query_ordinals(jax.random.fold_in(key_list[19], 71), 0)
    restored_ordinals = draw_restored_ordinals(jax.random.fold_in(key_list[19], 71), 0)
    symbols_following_snapshot = draw_symbols_following_snapshot(jax.random.fold_in(key_list[19], 71), 0)
    snapshot_summaries = gaussian(key_list[7], (REBUILDS, HEADS, PARTITION_LENGTH, PARTITION_LENGTH), 1.0, 6.0, ((0, 64), (1, 8)), jnp.float32)
    following_snapshot_features = gaussian(key_list[8], (REBUILDS, SPAN, MODEL_WIDTH), 1.0, 6.0, ((0, 64), (2, 8)))
    earlier_segment_feature = gaussian(key_list[9], (REBUILDS, MODEL_WIDTH), 1.0, 6.0, ((0, 64), (1, 8)))
    acceptor_coefficients = gaussian(key_list[10], (MODEL_WIDTH, LANE_COUNT), MODEL_WIDTH ** -0.5, 0.125, ((1, 8),))
    address_coefficients = gaussian(key_list[11], (MODEL_WIDTH, LANE_COUNT), MODEL_WIDTH ** -0.5, 0.125, ((1, 8),))
    payload_coefficients = gaussian(key_list[12], (MODEL_WIDTH, LANE_COUNT), MODEL_WIDTH ** -0.5, 0.125, ((1, 8),))
    lagged_interpolants = jnp.clip(jax.random.uniform(key_list[13], (4, MODEL_WIDTH), jnp.float32, 0.0, 1.0), 0.0, 1.0)
    fading_narrowing_matrix = gaussian(key_list[14], (MODEL_WIDTH, DECAY_RANK), MODEL_WIDTH ** -0.5, 0.125)
    fading_expanding_matrix = gaussian(key_list[15], (DECAY_RANK, LANE_COUNT), DECAY_RANK ** -0.5, 0.75, ((1, 8),))
    lane_fading_logit = jnp.clip(-6.0 + 5.0 * jax.random.uniform(key_list[16], (LANE_COUNT,), jnp.float32) ** levels(key_list[16], (LANE_COUNT,), ((0, 8),), -0.2, 0.2), -6.0, -1.0)
    present_step_reward = gaussian(key_list[17], (LANE_COUNT,), 0.5, 3.0, ((0, 8),), jnp.float32)
    cluster_scaling_vector = jnp.clip(1.0 + 0.18 * jax.random.normal(key_list[18], (LANE_COUNT,), jnp.float32), 0.1, 1.9)
    return dict(guessed_symbol_features=guessed_symbol_features, earlier_feature=earlier_feature, query_memory_summary=query_memory_summary, approved_guesses=approved_guesses, query_ordinals=query_ordinals, restored_ordinals=restored_ordinals, symbols_following_snapshot=symbols_following_snapshot, snapshot_summaries=snapshot_summaries, following_snapshot_features=following_snapshot_features, earlier_segment_feature=earlier_segment_feature, acceptor_coefficients=acceptor_coefficients, address_coefficients=address_coefficients, payload_coefficients=payload_coefficients, lagged_interpolants=lagged_interpolants, fading_narrowing_matrix=fading_narrowing_matrix, fading_expanding_matrix=fading_expanding_matrix, lane_fading_logit=lane_fading_logit, present_step_reward=present_step_reward, cluster_scaling_vector=cluster_scaling_vector)


NORM_EPS = 0.00064

def mixed_inputs(token_inputs, prior_state, lagged_interpolants):
    shifted = jnp.concatenate([prior_state[:, None, :], token_inputs[:, :-1, :]], axis=1)
    present_step = token_inputs.astype(jnp.float32)
    change = shifted.astype(jnp.float32) - present_step
    return [(present_step + change * lagged_interpolants[position]).astype(jnp.bfloat16) for position in range(4)]

def projection_weights(token_inputs, prior_state, receptance_gated_output, lagged_interpolants, acceptor_coefficients, address_coefficients, payload_coefficients, fading_narrowing_matrix, fading_expanding_matrix, lane_fading_logit):
    number, length, features = token_inputs.shape
    shift_blended = [member.reshape(number * length, features) for member in mixed_inputs(token_inputs, prior_state, lagged_interpolants)]
    address_mapped = jnp.dot(shift_blended[1], address_coefficients, preferred_element_type=jnp.float32)
    payload_mapped = jnp.dot(shift_blended[2], payload_coefficients, preferred_element_type=jnp.float32)
    decay_lowrank_term = jnp.tanh(jnp.dot(shift_blended[3], fading_narrowing_matrix, preferred_element_type=jnp.float32)).astype(jnp.bfloat16)
    fading_multiplier = jnp.exp(-jnp.exp(lane_fading_logit + jnp.dot(decay_lowrank_term, fading_expanding_matrix, preferred_element_type=jnp.float32)))
    results = [address_mapped, payload_mapped, fading_multiplier]
    if receptance_gated_output:
        results = [jnp.dot(shift_blended[0], acceptor_coefficients, preferred_element_type=jnp.float32)] + results
    return tuple((member.reshape(number, length, -1, PARTITION_LENGTH) for member in results))

def advance(initial_summary, address_mapped, payload_mapped, fading_multiplier, valid_mask):

    def update(running, inputs):
        present_address, present_payload, decay_now, valid_now = inputs
        advanced = decay_now[..., :, None] * running + present_address[..., :, None] * present_payload[..., None, :]
        return (jnp.where(valid_now[:, None, None, None], advanced, running), None)
    series = tuple((jnp.moveaxis(member, 1, 0) for member in (address_mapped, payload_mapped, fading_multiplier, valid_mask)))
    finished, _ = lax.scan(update, initial_summary, series)
    return finished

def confirm_guesses(initial_summary, acceptor_lines, address_mapped, payload_mapped, fading_multiplier, present_step_reward, approved_guesses):
    reward_for_partition = present_step_reward.reshape(-1, PARTITION_LENGTH)[None]

    def update(running, inputs):
        present_step, chosen_summary = running
        present_acceptor, present_address, present_payload, decay_now, position = inputs
        readout_vector = jnp.einsum('nhi,nhij->nhj', present_acceptor, present_step, precision=lax.Precision.HIGHEST)
        immediate_reward_part = lax.optimization_barrier(jnp.sum(present_acceptor * reward_for_partition * present_address, axis=-1, keepdims=True)) * present_payload
        present_step = decay_now[..., :, None] * present_step + present_address[..., :, None] * present_payload[..., None, :]
        chosen_summary = jnp.where((approved_guesses > position)[:, None, None, None], present_step, chosen_summary)
        return ((present_step, chosen_summary), readout_vector + immediate_reward_part)
    positions = jnp.arange(acceptor_lines.shape[1], dtype=jnp.int32)
    series = tuple((jnp.moveaxis(member, 1, 0) for member in (acceptor_lines, address_mapped, payload_mapped, fading_multiplier))) + (positions,)
    (_, chosen_summary), sublevel_results = lax.scan(update, (initial_summary, initial_summary), series)
    return (chosen_summary, jnp.moveaxis(sublevel_results, 0, 1))

def group_norm(sublevel_results, cluster_scaling_vector):
    centre = sublevel_results - lax.optimization_barrier(jnp.mean(sublevel_results, axis=-1, keepdims=True))
    spread = lax.optimization_barrier(jnp.mean(centre * centre, axis=-1, keepdims=True))
    normed = centre * lax.rsqrt(spread + NORM_EPS)
    flat = normed.reshape(normed.shape[0], normed.shape[1], -1)
    return (flat * cluster_scaling_vector).astype(jnp.bfloat16)

def reference(guessed_symbol_features, earlier_feature, query_memory_summary, approved_guesses, query_ordinals, restored_ordinals, symbols_following_snapshot, snapshot_summaries, following_snapshot_features, earlier_segment_feature, acceptor_coefficients, address_coefficients, payload_coefficients, lagged_interpolants, fading_narrowing_matrix, fading_expanding_matrix, lane_fading_logit, present_step_reward, cluster_scaling_vector):
    layer_weights = (lagged_interpolants, acceptor_coefficients, address_coefficients, payload_coefficients, fading_narrowing_matrix, fading_expanding_matrix, lane_fading_logit)
    span_key, span_value, span_decay = projection_weights(following_snapshot_features, earlier_segment_feature, False, *layer_weights)
    valid_mask = jnp.arange(SPAN, dtype=jnp.int32)[None, :] < symbols_following_snapshot[:, None]
    rebuilt = advance(snapshot_summaries, span_key, span_value, span_decay, valid_mask)
    matched = query_ordinals[None, :] == restored_ordinals[:, None]
    owner_index = lax.optimization_barrier(jnp.sum(jnp.where(matched, jnp.arange(REQUESTS, dtype=jnp.int32)[None, :], 0), axis=1)).astype(jnp.int32)
    initial_summary = query_memory_summary.at[owner_index].set(rebuilt)
    acceptor_lines, address_mapped, payload_mapped, fading_multiplier = projection_weights(guessed_symbol_features, earlier_feature, True, *layer_weights)
    chosen_summary, sublevel_results = confirm_guesses(initial_summary, acceptor_lines, address_mapped, payload_mapped, fading_multiplier, present_step_reward, approved_guesses)
    return (group_norm(sublevel_results, cluster_scaling_vector), chosen_summary)
```

```python
import jax
import jax.numpy as jnp
from jax import lax
from jax.experimental import pallas as pl
from jax.experimental.pallas import tpu as pltpu
from jax.sharding import PartitionSpec as P

MESH = pl.DeviceIdType.MESH
F32 = jnp.float32
BF16 = jnp.bfloat16

NX, NZ, NH = 4, 16, 8
NREQ = NX * NZ
T = 16
SPAN = 32
Q = 8
W = 2048
KS = W // NH
C = 128
HD = 64
ROWS = 72
NORM_EPS = 0.00064


def norm(o):
    return (o[0] % NX, o[1] % NZ)


def plan():
    first = [(0, 4), (0, -4), (0, 3), (0, -3), (0, 2), (0, -2), (0, 1), (0, -1)]
    second = [(-4, d) for d in (4, 3, 2, 1)] + [(4, d) for d in (-3, -2, -1)]
    stage1 = [((0, 0), norm(d)) for d in first]
    stage2 = [(norm((0, o)), norm((0, d))) for o, d in second]
    held1 = [(0, 0)] + [norm((0, -d[1])) for d in first]
    held2 = [norm((0, o - d)) for o, d in second]
    xs = [(2, 0), (1, 0), (3, 0)]
    return (
        stage1,
        stage2,
        [(o, d) for o in held1 for d in xs],
        [(o, d) for o in held2 for d in xs],
    )


STAGES = plan()
MOVES = STAGES[0] + STAGES[1] + STAGES[2] + STAGES[3]
LANDS = {norm((o[0] - d[0], o[1] - d[1])): i for i, (o, d) in enumerate(MOVES)}
PARTNERS = sorted({d for _, d in MOVES})


def split(x):
    hi = x.astype(BF16)
    return hi, (x - hi.astype(F32)).astype(BF16)


def dot(a, b):
    return jnp.dot(a, b, preferred_element_type=F32)


def dot_t(a, b):
    return lax.dot_general(a, b, (((0,), (0,)), ((), ())), preferred_element_type=F32)


def outer3(a, b):
    ah, al = split(a)
    bh, bl = split(b)
    return dot_t(ah, bh) + dot_t(ah, bl) + dot_t(al, bh)


def halves(m):
    lane = lax.broadcasted_iota(jnp.int32, (HD, C), 1)
    return jnp.where(lane < HD, m[:HD], m[HD:])


def mixes(cur, prev, mu):
    change = prev - cur
    return lambda m: (cur + change * mu[m : m + 1]).astype(BF16)


def decay_of(low, wn, we, logit):
    rank = jnp.tanh(dot(low, wn)).astype(BF16)
    return jnp.exp(-jnp.exp(logit + dot(rank, we)))


def kernel(
    approved_s, ordinal_s, restored_s, span_len_s,
    drafts_ref, earlier_ref, span_ref, span_prev_ref, mu_ref, we_ref, logit_ref, bonus_ref, gain_ref,
    state_hbm, snap_hbm, wr_hbm, wk_hbm, wv_hbm, wn_hbm,
    verified_ref, new_ref,
    state, snap, wr, wk, wv, wn,
    xs, xd, tmp, gathered, prods, rt, intra, kh, vv, kv_new,
    lsem, s_send, s_recv, d_send, d_recv, g_send, g_recv,
):
    req = lax.axis_index("req")
    me = lax.axis_index("head")
    mx, mz = req // NZ, lax.rem(req, NZ)

    def at(d):
        return lax.rem(mx + d[0], NX) * NZ + lax.rem(mz + d[1], NZ)

    local = [
        pltpu.make_async_copy(src, dst, lsem.at[i])
        for i, (src, dst) in enumerate(
            [(wk_hbm, wk), (wv_hbm, wv), (wn_hbm, wn), (snap_hbm, snap), (wr_hbm, wr), (state_hbm, state)]
        )
    ]
    for c in local:
        c.start()

    barrier = pltpu.get_barrier_semaphore()
    for k in range(1, NH):
        pl.semaphore_signal(barrier, inc=1, device_id=(req, lax.rem(me + k, NH)), device_id_type=MESH)
    for d in PARTNERS:
        pl.semaphore_signal(barrier, inc=1, device_id=(at(d), me), device_id_type=MESH)

    mine = pl.ds(pl.multiple_of(me * KS, KS), KS)
    prev8 = jnp.broadcast_to(span_prev_ref[...].astype(F32), (8, KS))
    xs[:, mine] = jnp.concatenate([prev8, span_ref[0].astype(F32)], axis=0).astype(BF16)
    for q in range(Q):
        tmp[0, pl.ds(q * T, T)] = drafts_ref[q, :, :C].astype(F32)
        tmp[1, pl.ds(q * T, T)] = drafts_ref[q, :, C:].astype(F32)
    turned = [jnp.concatenate([tmp[i, pl.ds(t, Q, stride=T)] for t in range(T)], axis=0) for i in range(2)]
    early = earlier_ref[...].astype(F32)
    xd[:, mine] = jnp.concatenate([early, jnp.concatenate(turned, axis=1)], axis=0).astype(BF16)

    pl.semaphore_wait(barrier, NH - 1 + len(PARTNERS))

    def spread(buf, send, recv, k, slot):
        ref = buf.at[:, pl.ds(pl.multiple_of(slot * KS, KS), KS)]
        return pltpu.make_async_remote_copy(
            src_ref=ref, dst_ref=ref, send_sem=send.at[k - 1], recv_sem=recv.at[k - 1],
            device_id=(req, lax.rem(me + k, NH)), device_id_type=MESH,
        )

    order = (4, 5, 3, 2, 6, 7, 1)
    for k in order:
        spread(xs, s_send, s_recv, k, me).start()
    for k in order:
        spread(xd, d_send, d_recv, k, me).start()
    for c in local[:4]:
        c.wait()
    mu = mu_ref[...]
    we = we_ref[...]
    logit = logit_ref[...]

    for k in order:
        spread(xs, s_send, s_recv, k, lax.rem(me + NH - k, NH)).wait_recv()
    both = xs[...].astype(F32)
    blend = mixes(both[8:], pltpu.roll(both, 1, axis=0)[8:], mu)
    key = dot(blend(1), wk[...])
    value = dot(blend(2), wv[...])
    decay = decay_of(blend(3), wn[...], we, logit)
    row = lax.broadcasted_iota(jnp.int32, (SPAN, C), 0)
    valid = row < span_len_s[0]
    key = jnp.where(valid, key, 0.0)
    tail = jnp.where(valid, decay, 1.0)
    for d in (1, 2, 4, 8, 16):
        tail = tail * jnp.where(row < SPAN - d, pltpu.roll(tail, SPAN - d, axis=0), 1.0)
    after = jnp.where(row < SPAN - 1, pltpu.roll(tail, SPAN - 1, axis=0), 1.0)
    whole = jnp.transpose(jnp.broadcast_to(tail[0:1], (8, C)))

    def column(m, q):
        return halves(jnp.broadcast_to(m[:, q : q + 1], (C, C)))

    def beside(ref_pair):
        return jnp.concatenate([ref_pair[0], ref_pair[1]], axis=1)

    rebuilt = column(whole, 0) * beside(snap[0]) + halves(outer3(key * after, value))
    gathered[req, pl.ds(0, HD)] = rebuilt.astype(BF16)
    place = (restored_s[0] - req * Q).astype(F32)
    gathered[req, pl.ds(HD, ROWS - HD)] = jnp.full((ROWS - HD, C), place, F32).astype(BF16)

    def move(i):
        o, d = MOVES[i]
        ref = gathered.at[at(o)]
        return pltpu.make_async_remote_copy(
            src_ref=ref, dst_ref=ref, send_sem=g_send.at[i], recv_sem=g_recv.at[i],
            device_id=(at(d), me), device_id_type=MESH,
        )

    def landed(i):
        o, d = MOVES[i]
        ref = gathered.at[at(norm((o[0] - d[0], o[1] - d[1])))]
        pltpu.make_async_remote_copy(
            src_ref=ref, dst_ref=ref, send_sem=g_send.at[i], recv_sem=g_recv.at[i],
            device_id=(at(d), me), device_id_type=MESH,
        ).wait_recv()

    n1, n2, n3, n4 = (len(s) for s in STAGES)
    for i in range(n1):
        move(i).start()
    for i in range(n1 + n2, n1 + n2 + 3):
        move(i).start()

    local[4].wait()
    local[5].wait()
    for k in order:
        spread(xd, d_send, d_recv, k, lax.rem(me + NH - k, NH)).wait_recv()
    both = xd[...].astype(F32)
    blend = mixes(both[Q:], both[:-Q], mu)
    r = dot(blend(0), wr[...]).reshape(T, Q, C)
    k = dot(blend(1), wk[...]).reshape(T, Q, C)
    v = dot(blend(2), wv[...]).reshape(T, Q, C)
    w = decay_of(blend(3), wn[...], we, logit).reshape(T, Q, C)

    for i in range(n1):
        landed(i)
    for i in range(n1, n1 + n2):
        move(i).start()
    for i in range(n1 + n2 + 3, n1 + n2 + n3):
        move(i).start()

    prods[pl.ds(0, T)] = r * bonus_ref[...].reshape(1, 1, C) * k
    run = r[1:]
    rt[pl.ds(0, Q)] = r[0]
    base = T
    bases = [0]
    for d in range(1, T):
        bases.append(base)
        prods[pl.ds(base, T - d)] = run * k[: T - d]
        base += T - d
        run = run * w[: T - d]
        rt[pl.ds(d * Q, Q)] = run[0]
        run = run[1:]
    lane_r = lax.broadcasted_iota(jnp.int32, (C, C), 0)
    lane_c = lax.broadcasted_iota(jnp.int32, (C, C), 1)
    ones = jnp.where((lane_r < HD) == (lane_c < HD), 1.0, 0.0).astype(BF16)
    ph, plo = split(prods[...].reshape(base * Q, C))
    scores = (dot(ph, ones) + dot(plo, ones)).reshape(base, Q, C)
    out = scores[0:T] * v
    acc = [out[t] for t in range(T)]
    for d in range(1, T):
        part = scores[bases[d] : bases[d] + T - d] * v[: T - d]
        for t in range(d, T):
            acc[t] = acc[t] + part[t - d]
    for t in range(T):
        intra[pl.ds(t * Q, Q)] = acc[t]

    sub = lax.broadcasted_iota(jnp.int32, (Q, C), 0)
    accepted = jnp.zeros((Q, C), jnp.int32)
    for q in range(Q):
        accepted = jnp.where(sub == q, approved_s[q], accepted)
    tail = jnp.ones((Q, C), F32)
    for t in range(T - 1, -1, -1):
        live = accepted > t
        kh[pl.ds(t * Q, Q)] = jnp.where(live, k[t], 0.0) * tail
        vv[pl.ds(t * Q, Q)] = v[t]
        tail = jnp.where(live, w[t], 1.0) * tail
    whole = jnp.transpose(tail)
    lane16 = lax.broadcasted_iota(jnp.int32, (T, C), 1)

    def per_query(ref, q):
        return ref[pl.ds(q, T, stride=Q)]

    for q in range(Q):
        kv_new[q] = halves(outer3(per_query(kh, q), per_query(vv, q)))

    for i in range(n1, n1 + n2):
        landed(i)
    for i in range(n1 + n2 + n3, len(MOVES)):
        move(i).start()
    for i in range(n1 + n2, len(MOVES)):
        landed(i)

    lane64 = lax.broadcasted_iota(jnp.int32, (HD, C), 1)
    outs = []
    for q in range(Q):
        ordinal = ordinal_s[q]
        entry = ordinal // Q
        block = gathered[entry].astype(F32)
        hit = block[HD : HD + 1] == (ordinal - entry * Q).astype(F32)
        start = jnp.where(hit, block[:HD], beside(state[q]))
        new = column(whole, q) * start + kv_new[q]
        new_ref[q, 0] = new[:, :HD]
        new_ref[q, 1] = new[:, HD:]
        rq = per_query(rt, q)
        left = jnp.concatenate([rq[:, :HD], rq[:, HD:]], axis=0)
        lh, ll = split(left)
        sh, sl = split(start)
        res = dot(lh, sh) + dot(lh, sl) + dot(ll, sh)
        outs.append(per_query(intra, q) + jnp.where(lane16 < HD, res[:T], res[T:]))
    full = jnp.concatenate(outs, axis=0)

    def head_mean(x):
        h, lo = split(x)
        return (dot(h, ones) + dot(lo, ones)) * (1.0 / HD)

    centre = full - head_mean(full)
    normed = centre * lax.rsqrt(head_mean(centre * centre) + NORM_EPS) * gain_ref[...]
    verified_ref[...] = normed.reshape(Q, T, C).astype(BF16)

    for k in order:
        spread(xs, s_send, s_recv, k, me).wait_send()
        spread(xd, d_send, d_recv, k, me).wait_send()
    for i in range(len(MOVES)):
        move(i).wait_send()


def per_device(
    drafts, earlier, state, approved, ordinals, restored, span_len, snap, span, span_prev,
    wr, wk, wv, mu, wn, we, logit, bonus, gain,
):
    smem = pl.BlockSpec(memory_space=pltpu.SMEM)
    vmem = pl.BlockSpec(memory_space=pltpu.VMEM)
    hbm = pl.BlockSpec(memory_space=pltpu.HBM)
    dma = pltpu.SemaphoreType.DMA
    n = len(MOVES)
    pairs = T * (T + 1) // 2
    return pl.pallas_call(
        kernel,
        out_shape=(
            jax.ShapeDtypeStruct((Q, T, C), BF16),
            jax.ShapeDtypeStruct((Q, 2, HD, HD), F32),
        ),
        in_specs=[smem] * 4 + [vmem] * 9 + [hbm] * 6,
        out_specs=(vmem, vmem),
        scratch_shapes=[
            pltpu.VMEM((Q, 2, HD, HD), F32),
            pltpu.VMEM((1, 2, HD, HD), F32),
            pltpu.VMEM((W, C), BF16),
            pltpu.VMEM((W, C), BF16),
            pltpu.VMEM((W, C), BF16),
            pltpu.VMEM((W, HD), BF16),
            pltpu.VMEM((8 + SPAN, W), BF16),
            pltpu.VMEM((Q + Q * T, W), BF16),
            pltpu.VMEM((2, Q * T, C), F32),
            pltpu.VMEM((NREQ, ROWS, C), BF16),
            pltpu.VMEM((pairs, Q, C), F32),
            pltpu.VMEM((T * Q, C), F32),
            pltpu.VMEM((T * Q, C), F32),
            pltpu.VMEM((T * Q, C), F32),
            pltpu.VMEM((T * Q, C), F32),
            pltpu.VMEM((Q, HD, C), F32),
            dma((6,)), dma((NH - 1,)), dma((NH - 1,)), dma((NH - 1,)), dma((NH - 1,)), dma((n,)), dma((n,)),
        ],
        compiler_params=pltpu.CompilerParams(
            collective_id=0, has_side_effects=True, vmem_limit_bytes=48 * 1024 * 1024
        ),
    )(
        approved, ordinals, restored, span_len,
        drafts, earlier, span, span_prev, mu, we, logit.reshape(1, C), bonus.reshape(1, C), gain.reshape(1, C),
        state, snap, wr, wk, wv, wn,
    )


def solution(mesh):
    in_specs = (
        P("req", None, "head"), P("req", "head"), P("req", "head", None, None), P("req"), P("req"), P("req"), P("req"),
        P("req", "head", None, None), P("req", None, "head"), P("req", "head"), P(None, "head"), P(None, "head"),
        P(None, "head"), P(), P(), P(None, "head"), P("head"), P("head"), P("head"),
    )
    out_specs = (P("req", None, "head"), P("req", "head", None, None))
    return jax.shard_map(per_device, mesh=mesh, in_specs=in_specs, out_specs=out_specs, check_vma=False)
```

```python
import jax
import jax.numpy as jnp
from jax import lax
from jax.experimental import pallas as pl
from jax.experimental.pallas import tpu as pltpu
from jax.sharding import PartitionSpec as P

MESH = pl.DeviceIdType.MESH
F32 = jnp.float32
BF16 = jnp.bfloat16

NX, NZ, NH = 4, 16, 8
T = 16
SPAN = 32
Q = 8
W = 2048
KS = W // NH
C = 128
HD = 64
ROWS = 72
NORM_EPS = 0.00064


FIRST = (4, -4, 3, -3, 2, -2, 1, -1)
SECOND = tuple((-4, d) for d in (4, 3, 2, 1)) + tuple((4, d) for d in (-3, -2, -1))
XS = (2, 1, 3)


def split(x):
    hi = x.astype(BF16)
    return hi, (x - hi.astype(F32)).astype(BF16)


def dot(a, b):
    return jnp.dot(a, b, preferred_element_type=F32)


def dot_t(a, b):
    return lax.dot_general(a, b, (((0,), (0,)), ((), ())), preferred_element_type=F32)


def outer3(a, b):
    ah, al = split(a)
    bh, bl = split(b)
    return dot_t(ah, bh) + dot_t(ah, bl) + dot_t(al, bh)


def halves(m):
    lane = lax.broadcasted_iota(jnp.int32, (HD, C), 1)
    return jnp.where(lane < HD, m[:HD], m[HD:])


def mixes(cur, prev, mu):
    change = prev - cur
    return lambda m: (cur + change * mu[m : m + 1]).astype(BF16)


def decay_of(low, wn, we, logit):
    low_rank = lax.dot_general(low, wn, (((1,), (1,)), ((), ())), preferred_element_type=F32)
    rank = jnp.tanh(low_rank).astype(BF16)
    return jnp.exp(-jnp.exp(logit + dot(rank, we)))


def kernel(
    approved_s, ordinal_s, restored_s, span_len_s,
    drafts_ref, earlier_ref, span_ref, span_prev_ref, mu_ref, we_ref, logit_ref, bonus_ref, gain_ref,
    state_hbm, snap_hbm, wr_hbm, wk_hbm, wv_hbm, wn_hbm,
    verified_ref, new_ref,
    state, snap, wr, wk, wv, wn,
    xs, xd, tmp, line, out_slots, in_slots, ord_v, ord_s,
    prods, rt, intra, kh, vv, kv_new, fade, lefts, base_out, base_new,
    lsem, s_send, s_recv, d_send, d_recv, z_send, z_far, z_near, z_last, x_send, x_recv, o_send, o_recv, o_sem,
):
    req = lax.axis_index("req")
    me = lax.axis_index("head")
    mx, mz = req // NZ, lax.rem(req, NZ)

    def along_z(d):
        return lax.rem(mz + (d % NZ), NZ)

    def along_x(d):
        return lax.rem(mx + d, NX)

    local = [
        pltpu.make_async_copy(src, dst, lsem.at[i])
        for i, (src, dst) in enumerate(
            [(wk_hbm, wk), (wv_hbm, wv), (wn_hbm, wn), (snap_hbm, snap), (wr_hbm, wr), (state_hbm, state)]
        )
    ]
    for c in local:
        c.start()

    barrier = pltpu.get_barrier_semaphore()
    for k in range(1, NH):
        pl.semaphore_signal(barrier, inc=1, device_id=(req, lax.rem(me + k, NH)), device_id_type=MESH)
    for d in FIRST:
        pl.semaphore_signal(barrier, inc=1, device_id=(mx * NZ + along_z(d), me), device_id_type=MESH)
    for d in XS:
        pl.semaphore_signal(barrier, inc=1, device_id=(along_x(d) * NZ + mz, me), device_id_type=MESH)

    mine = pl.ds(pl.multiple_of(me * KS, KS), KS)
    prev8 = jnp.broadcast_to(span_prev_ref[...].astype(F32), (8, KS))
    xs[:, mine] = jnp.concatenate([prev8, span_ref[0].astype(F32)], axis=0).astype(BF16)
    for q in range(Q):
        tmp[0, pl.ds(q * T, T)] = drafts_ref[q, :, :C].astype(F32)
        tmp[1, pl.ds(q * T, T)] = drafts_ref[q, :, C:].astype(F32)
    turned = [jnp.concatenate([tmp[i, pl.ds(t, Q, stride=T)] for t in range(T)], axis=0) for i in range(2)]
    early = earlier_ref[...].astype(F32)
    xd[:, mine] = jnp.concatenate([early, jnp.concatenate(turned, axis=1)], axis=0).astype(BF16)
    sub = lax.broadcasted_iota(jnp.int32, (Q, C), 0)
    accepted = jnp.zeros((Q, C), jnp.int32)
    ordinals = jnp.zeros((Q, C), jnp.int32)
    for q in range(Q):
        accepted = jnp.where(sub == q, approved_s[q], accepted)
        ordinals = jnp.where(sub == q, ordinal_s[q], ordinals)
    ord_v[mx] = ordinals

    pl.semaphore_wait(barrier, NH - 1 + len(FIRST) + len(XS))

    def spread(buf, send, recv, k, slot):
        ref = buf.at[:, pl.ds(pl.multiple_of(slot * KS, KS), KS)]
        return pltpu.make_async_remote_copy(
            src_ref=ref, dst_ref=ref, send_sem=send.at[k - 1], recv_sem=recv.at[k - 1],
            device_id=(req, lax.rem(me + k, NH)), device_id_type=MESH,
        )

    def tell(i, slot):
        ref = ord_v.at[slot]
        return pltpu.make_async_remote_copy(
            src_ref=ref, dst_ref=ref, send_sem=o_send.at[i], recv_sem=o_recv.at[i],
            device_id=(along_x(XS[i]) * NZ + mz, me), device_id_type=MESH,
        )

    order = (4, 5, 3, 2, 6, 7, 1)
    for k in order:
        spread(xs, s_send, s_recv, k, me).start()
    for i in range(len(XS)):
        tell(i, mx).start()
    for c in local[:4]:
        c.wait()
    mu = mu_ref[...]
    we = we_ref[...]
    logit = logit_ref[...]

    for k in order:
        spread(xs, s_send, s_recv, k, lax.rem(me + NH - k, NH)).wait_recv()
    for k in order:
        spread(xd, d_send, d_recv, k, me).start()
    both = xs[...].astype(F32)
    blend = mixes(both[8:], pltpu.roll(both, 1, axis=0)[8:], mu)
    key = dot(blend(1), wk[...])
    value = dot(blend(2), wv[...])
    decay = decay_of(blend(3), wn[...], we, logit)
    row = lax.broadcasted_iota(jnp.int32, (SPAN, C), 0)
    valid = row < span_len_s[0]
    key = jnp.where(valid, key, 0.0)
    tail = jnp.where(valid, decay, 1.0)
    for d in (1, 2, 4, 8, 16):
        tail = tail * jnp.where(row < SPAN - d, pltpu.roll(tail, SPAN - d, axis=0), 1.0)
    after = jnp.where(row < SPAN - 1, pltpu.roll(tail, SPAN - 1, axis=0), 1.0)
    whole = jnp.transpose(jnp.broadcast_to(tail[0:1], (8, C)))

    def column(m, q):
        return halves(jnp.broadcast_to(m[:, q : q + 1], (C, C)))

    def beside(ref_pair):
        return jnp.concatenate([ref_pair[0], ref_pair[1]], axis=1)

    rebuilt = column(whole, 0) * beside(snap[0]) + halves(outer3(key * after, value))
    line[mz, pl.ds(0, HD)] = rebuilt.astype(BF16)
    place = (restored_s[0] - req * Q).astype(F32)
    line[mz, pl.ds(HD, ROWS - HD)] = jnp.full((ROWS - HD, C), place, F32).astype(BF16)

    def hop(i, origin, d, sem):
        ref = line.at[along_z(origin)]
        return pltpu.make_async_remote_copy(
            src_ref=ref, dst_ref=ref, send_sem=z_send.at[i], recv_sem=sem,
            device_id=(mx * NZ + along_z(d), me), device_id_type=MESH,
        )

    first = [hop(i, 0, d, z_far.at[i] if i < 2 else z_near.at[i - 2]) for i, d in enumerate(FIRST)]
    second = [hop(len(FIRST) + i, o, d, z_last.at[i]) for i, (o, d) in enumerate(SECOND)]
    for c in first:
        c.start()

    local[4].wait()
    local[5].wait()
    for k in order:
        spread(xd, d_send, d_recv, k, lax.rem(me + NH - k, NH)).wait_recv()
    both = xd[...].astype(F32)
    blend = mixes(both[Q:], both[:-Q], mu)
    w = decay_of(blend(3), wn[...], we, logit).reshape(T, Q, C)
    k = dot(blend(1), wk[...]).reshape(T, Q, C)

    for i in range(2):
        hop(i, -FIRST[i], FIRST[i], z_far.at[i]).wait_recv()
    for c in second:
        c.start()

    v = dot(blend(2), wv[...]).reshape(T, Q, C)
    r = dot(blend(0), wr[...]).reshape(T, Q, C)

    prods[pl.ds(0, T)] = r * bonus_ref[...].reshape(1, 1, C) * k
    run = r[1:]
    rt[pl.ds(0, Q)] = r[0]
    base = T
    bases = [0]
    for d in range(1, T):
        bases.append(base)
        prods[pl.ds(base, T - d)] = run * k[: T - d]
        base += T - d
        run = run * w[: T - d]
        rt[pl.ds(d * Q, Q)] = run[0]
        run = run[1:]
    lane_r = lax.broadcasted_iota(jnp.int32, (C, C), 0)
    lane_c = lax.broadcasted_iota(jnp.int32, (C, C), 1)
    ones = jnp.where((lane_r < HD) == (lane_c < HD), 1.0, 0.0).astype(BF16)
    ph, plo = split(prods[...].reshape(base * Q, C))
    scores = (dot(ph, ones) + dot(plo, ones)).reshape(base, Q, C)
    out = scores[0:T] * v
    acc = [out[t] for t in range(T)]
    for d in range(1, T):
        part = scores[bases[d] : bases[d] + T - d] * v[: T - d]
        for t in range(d, T):
            acc[t] = acc[t] + part[t - d]
    for t in range(T):
        intra[pl.ds(t * Q, Q)] = acc[t]

    tail = jnp.ones((Q, C), F32)
    for t in range(T - 1, -1, -1):
        live = accepted > t
        kh[pl.ds(t * Q, Q)] = jnp.where(live, k[t], 0.0) * tail
        vv[pl.ds(t * Q, Q)] = v[t]
        tail = jnp.where(live, w[t], 1.0) * tail
    whole = jnp.transpose(tail)
    lane16 = lax.broadcasted_iota(jnp.int32, (T, C), 1)

    def pick(res):
        both = res[: 2 * T] + res[2 * T :]
        return jnp.where(lane16 < HD, both[:T], both[T:])

    for i in range(len(XS)):
        tell(i, along_x(NX - XS[i])).wait_recv()
    read = pltpu.make_async_copy(ord_v, ord_s, o_sem)
    read.start()

    for q in range(Q):
        mine_q = pl.ds(q, T, stride=Q)
        kv = halves(outer3(kh[mine_q], vv[mine_q]))
        col = column(whole, q)
        start = beside(state[q])
        kv_new[q] = kv
        fade[q] = col
        base_new[q] = col * start + kv
        rq = rt[mine_q]
        lh, ll = split(jnp.concatenate([rq[:, :HD], rq[:, HD:]], axis=0))
        left = jnp.concatenate([lh, ll], axis=0)
        lefts[q] = left
        sh, sl = split(start)
        zero = jnp.zeros((2 * T, C), F32)
        res = dot(left, sh) + jnp.concatenate([dot(lh, sl), zero], axis=0)
        base_out[q] = pick(res)
    read.wait()

    for i in range(len(FIRST) - 2):
        hop(i + 2, -FIRST[i + 2], FIRST[i + 2], z_near.at[i]).wait_recv()
    for i, (o, d) in enumerate(SECOND):
        hop(len(FIRST) + i, o - d, d, z_last.at[i]).wait_recv()

    def cross(i, slot):
        return pltpu.make_async_remote_copy(
            src_ref=out_slots.at[i], dst_ref=in_slots.at[slot], send_sem=x_send.at[i], recv_sem=x_recv.at[i],
            device_id=(along_x(XS[i]) * NZ + mz, me), device_id_type=MESH,
        )

    for i in range(len(XS)):
        for q in range(Q):
            out_slots[i, q] = line[lax.rem(ord_s[along_x(XS[i]), q, 0] // Q, NZ)]
        cross(i, mx).start()
    for q in range(Q):
        in_slots[mx, q] = line[lax.rem(ordinal_s[q] // Q, NZ)]
    for i in range(len(XS)):
        cross(i, along_x(NX - XS[i])).wait_recv()

    outs = []
    for q in range(Q):
        entry = ordinal_s[q] // Q
        block = in_slots[entry // NZ, q]
        body = block[:HD]
        hit = block[HD : HD + 1].astype(F32) == (ordinal_s[q] - entry * Q).astype(F32)
        new = jnp.where(hit, fade[q] * body.astype(F32) + kv_new[q], base_new[q])
        new_ref[q, 0] = new[:, :HD]
        new_ref[q, 1] = new[:, HD:]
        res = pick(dot(lefts[q], body))
        outs.append(intra[pl.ds(q, T, stride=Q)] + jnp.where(hit, res, base_out[q]))
    full = jnp.concatenate(outs, axis=0)

    def head_mean(x):
        h, lo = split(x)
        return (dot(h, ones) + dot(lo, ones)) * (1.0 / HD)

    centre = full - head_mean(full)
    normed = centre * lax.rsqrt(head_mean(centre * centre) + NORM_EPS) * gain_ref[...]
    verified_ref[...] = normed.reshape(Q, T, C).astype(BF16)

    for k in order:
        spread(xs, s_send, s_recv, k, me).wait_send()
        spread(xd, d_send, d_recv, k, me).wait_send()
    for c in first + second:
        c.wait_send()
    for i in range(len(XS)):
        tell(i, mx).wait_send()
        cross(i, mx).wait_send()


def per_device(
    drafts, earlier, state, approved, ordinals, restored, span_len, snap, span, span_prev,
    wr, wk, wv, mu, wn, we, logit, bonus, gain,
):
    smem = pl.BlockSpec(memory_space=pltpu.SMEM)
    vmem = pl.BlockSpec(memory_space=pltpu.VMEM)
    hbm = pl.BlockSpec(memory_space=pltpu.HBM)
    dma = pltpu.SemaphoreType.DMA
    pairs = T * (T + 1) // 2
    return pl.pallas_call(
        kernel,
        out_shape=(
            jax.ShapeDtypeStruct((Q, T, C), BF16),
            jax.ShapeDtypeStruct((Q, 2, HD, HD), F32),
        ),
        in_specs=[smem] * 4 + [vmem] * 9 + [hbm] * 6,
        out_specs=(vmem, vmem),
        scratch_shapes=[
            pltpu.VMEM((Q, 2, HD, HD), F32),
            pltpu.VMEM((1, 2, HD, HD), F32),
            pltpu.VMEM((W, C), BF16),
            pltpu.VMEM((W, C), BF16),
            pltpu.VMEM((W, C), BF16),
            pltpu.VMEM((HD, W), BF16),
            pltpu.VMEM((8 + SPAN, W), BF16),
            pltpu.VMEM((Q + Q * T, W), BF16),
            pltpu.VMEM((2, Q * T, C), F32),
            pltpu.VMEM((NZ, ROWS, C), BF16),
            pltpu.VMEM((len(XS), Q, ROWS, C), BF16),
            pltpu.VMEM((NX, Q, ROWS, C), BF16),
            pltpu.VMEM((NX, Q, C), jnp.int32),
            pltpu.SMEM((NX, Q, C), jnp.int32),
            pltpu.VMEM((pairs, Q, C), F32),
            pltpu.VMEM((T * Q, C), F32),
            pltpu.VMEM((T * Q, C), F32),
            pltpu.VMEM((T * Q, C), F32),
            pltpu.VMEM((T * Q, C), F32),
            pltpu.VMEM((Q, HD, C), F32),
            pltpu.VMEM((Q, HD, C), F32),
            pltpu.VMEM((Q, 4 * T, HD), BF16),
            pltpu.VMEM((Q, T, C), F32),
            pltpu.VMEM((Q, HD, C), F32),
            dma((6,)), dma((NH - 1,)), dma((NH - 1,)), dma((NH - 1,)), dma((NH - 1,)),
            dma((len(FIRST) + len(SECOND),)), dma((2,)), dma((len(FIRST) - 2,)), dma((len(SECOND),)),
            dma((len(XS),)), dma((len(XS),)), dma((len(XS),)), dma((len(XS),)), dma,
        ],
        compiler_params=pltpu.CompilerParams(
            collective_id=0, has_side_effects=True, vmem_limit_bytes=60 * 1024 * 1024
        ),
    )(
        approved, ordinals, restored, span_len,
        drafts, earlier, span, span_prev, mu, we, logit.reshape(1, C), bonus.reshape(1, C), gain.reshape(1, C),
        state, snap, wr, wk, wv, wn.T,
    )


def solution(mesh):
    in_specs = (
        P("req", None, "head"), P("req", "head"), P("req", "head", None, None), P("req"), P("req"), P("req"), P("req"),
        P("req", "head", None, None), P("req", None, "head"), P("req", "head"), P(None, "head"), P(None, "head"),
        P(None, "head"), P(), P(), P(None, "head"), P("head"), P("head"), P("head"),
    )
    out_specs = (P("req", None, "head"), P("req", "head", None, None))
    return jax.shard_map(per_device, mesh=mesh, in_specs=in_specs, out_specs=out_specs, check_vma=False)
```

```python
import jax
import jax.numpy as jnp
from jax import lax
from jax.experimental import pallas as pl
from jax.experimental.pallas import tpu as pltpu
from jax.sharding import PartitionSpec as P

MESH = pl.DeviceIdType.MESH
F32 = jnp.float32
BF16 = jnp.bfloat16

NX, NZ, NH = 4, 16, 8
T = 16
SPAN = 32
Q = 8
W = 2048
KS = W // NH
C = 128
HD = 64
ROWS = 72
NORM_EPS = 0.00064


GIVEN = 19
R = 4
FIRST = tuple(d for i in range(R, 0, -1) for d in (i, -i))
SECOND = tuple((-R, d) for d in range(8 - R, 0, -1)) + tuple((R, -d) for d in range(7 - R, 0, -1))
XS = (2, 1, 3)


PARTS = ((R, 1), (0, R), (R + 1, R), (2 * R + 1, NZ - 2 * R - 1))


def slot(rel):
    return (rel + R) % NZ


def split(x):
    hi = x.astype(BF16)
    return hi, (x - hi.astype(F32)).astype(BF16)


def dot(a, b):
    return jnp.dot(a, b, preferred_element_type=F32)


def dot_t(a, b):
    return lax.dot_general(a, b, (((0,), (0,)), ((), ())), preferred_element_type=F32)


def outer3(a, b):
    ah, al = split(a)
    bh, bl = split(b)
    return dot_t(ah, bh) + dot_t(ah, bl) + dot_t(al, bh)


def halves(m):
    lane = lax.broadcasted_iota(jnp.int32, (HD, C), 1)
    return jnp.where(lane < HD, m[:HD], m[HD:])


def mixes(cur, prev, mu):
    change = prev - cur
    return lambda m: (cur + change * mu[m : m + 1]).astype(BF16)


def decay_of(low, wn, we, logit):
    low_rank = lax.dot_general(low, wn, (((1,), (1,)), ((), ())), preferred_element_type=F32)
    rank = jnp.tanh(low_rank).astype(BF16)
    return jnp.exp(-jnp.exp(logit + dot(rank, we)))


def kernel(*refs):
    given, (verified_ref, new_ref), refs = refs[:GIVEN], refs[GIVEN : GIVEN + 2], refs[GIVEN + 2 :]
    held, refs = refs[:GIVEN], refs[GIVEN:]
    (
        span_ref, span_prev_ref, drafts_ref, earlier_ref, ordinal_s, approved_s, _, _,
        mu_ref, wk, wv, wn, we_ref, logit_ref, snap, wr, state, bonus_ref, gain_ref,
    ) = held
    restored_s, span_len_s = given[6:8]
    (
    xs, xd, tmp, blocks,
    prods, rt, intra, kh, vv, kv_new, fade, lefts, base_out, base_new,
    lsem, s_send, s_recv, d_send, d_recv, z_send, z_recv, x_send, x_recv,
    ) = refs
    req = lax.axis_index("req")
    me = lax.axis_index("head")
    mx, mz = req // NZ, lax.rem(req, NZ)

    def along_z(d):
        return lax.rem(mz + (d % NZ), NZ)

    def along_x(d):
        return lax.rem(mx + d, NX)

    barrier = pltpu.get_barrier_semaphore()
    for d in FIRST:
        pl.semaphore_signal(barrier, inc=1, device_id=(mx * NZ + along_z(d), me), device_id_type=MESH)
    for k in range(1, NH):
        pl.semaphore_signal(barrier, inc=1, device_id=(req, lax.rem(me + k, NH)), device_id_type=MESH)
    for d in XS:
        pl.semaphore_signal(barrier, inc=1, device_id=(along_x(d) * NZ + mz, me), device_id_type=MESH)

    local = [pltpu.make_async_copy(src, dst, lsem.at[i]) for i, (src, dst) in enumerate(zip(given, held)) if src.shape != (1,)]
    for c in local:
        c.start()
    for c in local[:2]:
        c.wait()
    mine = pl.ds(pl.multiple_of(me * KS, KS), KS)
    prev8 = jnp.broadcast_to(span_prev_ref[...].astype(F32), (8, KS))
    xs[:, mine] = jnp.concatenate([prev8, span_ref[0].astype(F32)], axis=0).astype(BF16)

    pl.semaphore_wait(barrier, NH - 1 + len(FIRST) + len(XS))

    def spread(buf, send, recv, k, slot):
        ref = buf.at[:, pl.ds(pl.multiple_of(slot * KS, KS), KS)]
        return pltpu.make_async_remote_copy(
            src_ref=ref, dst_ref=ref, send_sem=send.at[k - 1], recv_sem=recv.at[k - 1],
            device_id=(req, lax.rem(me + k, NH)), device_id_type=MESH,
        )

    order = (4, 5, 3, 2, 6, 7, 1)
    for k in order:
        spread(xs, s_send, s_recv, k, me).start()
    for c in local[2:6]:
        c.wait()
    for q in range(Q):
        tmp[0, pl.ds(q * T, T)] = drafts_ref[q, :, :C].astype(F32)
        tmp[1, pl.ds(q * T, T)] = drafts_ref[q, :, C:].astype(F32)
    turned = [jnp.concatenate([tmp[i, pl.ds(t, Q, stride=T)] for t in range(T)], axis=0) for i in range(2)]
    early = earlier_ref[...].astype(F32)
    xd[:, mine] = jnp.concatenate([early, jnp.concatenate(turned, axis=1)], axis=0).astype(BF16)
    sub = lax.broadcasted_iota(jnp.int32, (Q, C), 0)
    accepted = jnp.zeros((Q, C), jnp.int32)
    for q in range(Q):
        accepted = jnp.where(sub == q, approved_s[q], accepted)
    for c in local[6:]:
        c.wait()
    mu = mu_ref[...]
    we = we_ref[...]
    logit = logit_ref[...]

    for k in order:
        spread(xs, s_send, s_recv, k, lax.rem(me + NH - k, NH)).wait_recv()
    for k in order:
        spread(xd, d_send, d_recv, k, me).start()
    both = xs[...].astype(F32)
    blend = mixes(both[8:], pltpu.roll(both, 1, axis=0)[8:], mu)
    key = dot(blend(1), wk[...])
    value = dot(blend(2), wv[...])
    decay = decay_of(blend(3), wn[...], we, logit)
    row = lax.broadcasted_iota(jnp.int32, (SPAN, C), 0)
    valid = row < span_len_s[0]
    key = jnp.where(valid, key, 0.0)
    tail = jnp.where(valid, decay, 1.0)
    for d in (1, 2, 4, 8, 16):
        tail = tail * jnp.where(row < SPAN - d, pltpu.roll(tail, SPAN - d, axis=0), 1.0)
    after = jnp.where(row < SPAN - 1, pltpu.roll(tail, SPAN - 1, axis=0), 1.0)
    whole = jnp.transpose(jnp.broadcast_to(tail[0:1], (8, C)))

    def column(m, q):
        return halves(jnp.broadcast_to(m[:, q : q + 1], (C, C)))

    def beside(ref_pair):
        return jnp.concatenate([ref_pair[0], ref_pair[1]], axis=1)

    rebuilt = column(whole, 0) * beside(snap[0]) + halves(outer3(key * after, value))
    blocks[0, slot(0), pl.ds(0, HD)] = rebuilt.astype(BF16)
    place = (restored_s[0] - req * Q).astype(F32)
    blocks[0, slot(0), pl.ds(HD, ROWS - HD)] = jnp.full((ROWS - HD, C), place, F32).astype(BF16)

    def hop(i, origin, d, sem):
        return pltpu.make_async_remote_copy(
            src_ref=blocks.at[0, slot(origin)], dst_ref=blocks.at[0, slot(origin - d)],
            send_sem=z_send.at[i], recv_sem=sem,
            device_id=(mx * NZ + along_z(d), me), device_id_type=MESH,
        )

    def cross(i, part):
        span = pl.ds(*PARTS[part])
        return pltpu.make_async_remote_copy(
            src_ref=blocks.at[0, span], dst_ref=blocks.at[NX - XS[i], span],
            send_sem=x_send.at[part, i], recv_sem=x_recv.at[part, i],
            device_id=(along_x(XS[i]) * NZ + mz, me), device_id_type=MESH,
        )

    def land(i, rel):
        ref = blocks.at[0, slot(rel)]
        pltpu.make_async_remote_copy(
            src_ref=ref, dst_ref=ref, send_sem=z_send.at[i], recv_sem=z_recv.at[i],
            device_id=(mx * NZ + along_z(1), me), device_id_type=MESH,
        ).wait_recv()

    n1, n2 = len(FIRST), len(SECOND)
    moves = [hop(i, 0, d, z_recv.at[i]) for i, d in enumerate(FIRST)]
    moves += [cross(i, 0) for i in range(len(XS))]
    for c in moves:
        c.start()
    for i in range(2):
        land(i, -FIRST[i])
    second = [hop(n1 + i, o, d, z_recv.at[n1 + i]) for i, (o, d) in enumerate(SECOND)]
    for c in second:
        c.start()
    for i in range(2, n1):
        land(i, -FIRST[i])
    soon = [cross(i, part) for part in (1, 2) for i in range(len(XS))]
    for c in soon:
        c.start()

    for k in order:
        spread(xd, d_send, d_recv, k, lax.rem(me + NH - k, NH)).wait_recv()
    both = xd[...].astype(F32)
    blend = mixes(both[Q:], both[:-Q], mu)
    w = decay_of(blend(3), wn[...], we, logit).reshape(T, Q, C)
    k = dot(blend(1), wk[...]).reshape(T, Q, C)

    v = dot(blend(2), wv[...]).reshape(T, Q, C)
    r = dot(blend(0), wr[...]).reshape(T, Q, C)

    prods[pl.ds(0, T)] = r * bonus_ref[...].reshape(1, 1, C) * k
    run = r[1:]
    rt[pl.ds(0, Q)] = r[0]
    base = T
    bases = [0]
    for d in range(1, T):
        bases.append(base)
        prods[pl.ds(base, T - d)] = run * k[: T - d]
        base += T - d
        run = run * w[: T - d]
        rt[pl.ds(d * Q, Q)] = run[0]
        run = run[1:]
    lane_r = lax.broadcasted_iota(jnp.int32, (C, C), 0)
    lane_c = lax.broadcasted_iota(jnp.int32, (C, C), 1)
    ones = jnp.where((lane_r < HD) == (lane_c < HD), 1.0, 0.0).astype(BF16)
    ph, plo = split(prods[...].reshape(base * Q, C))
    scores = (dot(ph, ones) + dot(plo, ones)).reshape(base, Q, C)
    out = scores[0:T] * v
    acc = [out[t] for t in range(T)]
    for d in range(1, T):
        part = scores[bases[d] : bases[d] + T - d] * v[: T - d]
        for t in range(d, T):
            acc[t] = acc[t] + part[t - d]
    for t in range(T):
        intra[pl.ds(t * Q, Q)] = acc[t]

    tail = jnp.ones((Q, C), F32)
    for t in range(T - 1, -1, -1):
        live = accepted > t
        kh[pl.ds(t * Q, Q)] = jnp.where(live, k[t], 0.0) * tail
        vv[pl.ds(t * Q, Q)] = v[t]
        tail = jnp.where(live, w[t], 1.0) * tail
    whole = jnp.transpose(tail)
    lane16 = lax.broadcasted_iota(jnp.int32, (T, C), 1)

    def pick(res):
        both = res[: 2 * T] + res[2 * T :]
        return jnp.where(lane16 < HD, both[:T], both[T:])

    for q in range(Q):
        mine_q = pl.ds(q, T, stride=Q)
        kv = halves(outer3(kh[mine_q], vv[mine_q]))
        col = column(whole, q)
        start = beside(state[q])
        kv_new[q] = kv
        fade[q] = col
        base_new[q] = col * start + kv
        rq = rt[mine_q]
        lh, ll = split(jnp.concatenate([rq[:, :HD], rq[:, HD:]], axis=0))
        left = jnp.concatenate([lh, ll], axis=0)
        lefts[q] = left
        sh, sl = split(start)
        zero = jnp.zeros((2 * T, C), F32)
        res = dot(left, sh) + jnp.concatenate([dot(lh, sl), zero], axis=0)
        base_out[q] = pick(res)
    for i in range(n2):
        land(n1 + i, SECOND[i][0] - SECOND[i][1])
    late = [cross(i, 3) for i in range(len(XS))]
    for c in late:
        c.start()
    for i in range(len(XS)):
        for part in range(len(PARTS)):
            cross(i, part).wait_recv()

    outs = []
    for q in range(Q):
        entry = ordinal_s[q] // Q
        block = blocks[lax.rem(entry // NZ + NX - mx, NX), lax.rem(entry + (NZ + R) - mz, NZ)]
        body = block[:HD]
        hit = block[HD : HD + 1].astype(F32) == (ordinal_s[q] - entry * Q).astype(F32)
        new = jnp.where(hit, fade[q] * body.astype(F32) + kv_new[q], base_new[q])
        new_ref[q, 0] = new[:, :HD]
        new_ref[q, 1] = new[:, HD:]
        res = pick(dot(lefts[q], body))
        outs.append(intra[pl.ds(q, T, stride=Q)] + jnp.where(hit, res, base_out[q]))
    full = jnp.concatenate(outs, axis=0)

    def head_mean(x):
        h, lo = split(x)
        return (dot(h, ones) + dot(lo, ones)) * (1.0 / HD)

    centre = full - head_mean(full)
    normed = centre * lax.rsqrt(head_mean(centre * centre) + NORM_EPS) * gain_ref[...]
    verified_ref[...] = normed.reshape(Q, T, C).astype(BF16)

    for k in order:
        spread(xs, s_send, s_recv, k, me).wait_send()
        spread(xd, d_send, d_recv, k, me).wait_send()
    for c in moves + second + soon + late:
        c.wait_send()


def per_device(
    drafts, earlier, state, approved, ordinals, restored, span_len, snap, span, span_prev,
    wr, wk, wv, mu, wn, we, logit, bonus, gain,
):
    given = [
        span, span_prev, drafts, earlier, ordinals, approved, restored, span_len,
        mu, wk, wv, wn.T, we, logit.reshape(1, C), snap, wr, state, bonus.reshape(1, C), gain.reshape(1, C),
    ]
    given = [x if x.size == 1 else pltpu.with_memory_space_constraint(x, pltpu.HBM) for x in given]
    held = [pltpu.SMEM(x.shape, x.dtype) if x.dtype == jnp.int32 else pltpu.VMEM(x.shape, x.dtype) for x in given]
    vmem = pl.BlockSpec(memory_space=pltpu.VMEM)
    dma = pltpu.SemaphoreType.DMA
    pairs = T * (T + 1) // 2
    return pl.pallas_call(
        kernel,
        out_shape=(
            jax.ShapeDtypeStruct((Q, T, C), BF16),
            jax.ShapeDtypeStruct((Q, 2, HD, HD), F32),
        ),
        in_specs=[pl.BlockSpec(memory_space=pltpu.SMEM if x.size == 1 else pltpu.HBM) for x in given],
        out_specs=(vmem, vmem),
        scratch_shapes=held
        + [
            pltpu.VMEM((8 + SPAN, W), BF16),
            pltpu.VMEM((Q + Q * T, W), BF16),
            pltpu.VMEM((2, Q * T, C), F32),
            pltpu.VMEM((NX, NZ, ROWS, C), BF16),
            pltpu.VMEM((pairs, Q, C), F32),
            pltpu.VMEM((T * Q, C), F32),
            pltpu.VMEM((T * Q, C), F32),
            pltpu.VMEM((T * Q, C), F32),
            pltpu.VMEM((T * Q, C), F32),
            pltpu.VMEM((Q, HD, C), F32),
            pltpu.VMEM((Q, HD, C), F32),
            pltpu.VMEM((Q, 4 * T, HD), BF16),
            pltpu.VMEM((Q, T, C), F32),
            pltpu.VMEM((Q, HD, C), F32),
            dma((GIVEN,)), dma((NH - 1,)), dma((NH - 1,)), dma((NH - 1,)), dma((NH - 1,)),
            dma((NZ - 1,)), dma((NZ - 1,)), dma((len(PARTS), len(XS))), dma((len(PARTS), len(XS))),
        ],
        compiler_params=pltpu.CompilerParams(
            collective_id=0, has_side_effects=True, vmem_limit_bytes=32 * 1024 * 1024
        ),
    )(*given)


def solution(mesh):
    in_specs = (
        P("req", None, "head"), P("req", "head"), P("req", "head", None, None), P("req"), P("req"), P("req"), P("req"),
        P("req", "head", None, None), P("req", None, "head"), P("req", "head"), P(None, "head"), P(None, "head"),
        P(None, "head"), P(), P(), P(None, "head"), P("head"), P("head"), P("head"),
    )
    out_specs = (P("req", None, "head"), P("req", "head", None, None))
    return jax.shard_map(per_device, mesh=mesh, in_specs=in_specs, out_specs=out_specs, check_vma=False)
```

```python
import jax
import jax.numpy as jnp
from jax import lax
from jax.experimental import pallas as pl
from jax.experimental.pallas import tpu as pltpu
from jax.sharding import PartitionSpec as P

MESH = pl.DeviceIdType.MESH
F32 = jnp.float32
BF16 = jnp.bfloat16

NX, NZ, NH = 4, 16, 8
T = 16
SPAN = 32
Q = 8
W = 2048
KS = W // NH
C = 128
HD = 64
ROWS = 72
NORM_EPS = 0.00064


GIVEN = 19
R = 4
FIRST = tuple(d for i in range(R, 0, -1) for d in (i, -i))
SECOND = tuple((-R, d) for d in range(8 - R, 0, -1)) + tuple((R, -d) for d in range(7 - R, 0, -1))
XS = (2, 1, 3)


PACK = Q * HD + 8


def slot(rel):
    return (rel + R) % NZ


def split(x):
    hi = x.astype(BF16)
    return hi, (x - hi.astype(F32)).astype(BF16)


def dot(a, b):
    return jnp.dot(a, b, preferred_element_type=F32)


def dot_t(a, b):
    return lax.dot_general(a, b, (((0,), (0,)), ((), ())), preferred_element_type=F32)


def outer3(a, b):
    ah, al = split(a)
    bh, bl = split(b)
    return dot_t(ah, bh) + dot_t(ah, bl) + dot_t(al, bh)


def halves(m):
    lane = lax.broadcasted_iota(jnp.int32, (HD, C), 1)
    return jnp.where(lane < HD, m[:HD], m[HD:])


def mixes(cur, prev, mu):
    change = prev - cur
    return lambda m: (cur + change * mu[m : m + 1]).astype(BF16)


def decay_of(low, wn, we, logit):
    low_rank = lax.dot_general(low, wn, (((1,), (1,)), ((), ())), preferred_element_type=F32)
    rank = jnp.tanh(low_rank).astype(BF16)
    return jnp.exp(-jnp.exp(logit + dot(rank, we)))


def kernel(*refs):
    given, (verified_ref, new_ref), refs = refs[:GIVEN], refs[GIVEN : GIVEN + 2], refs[GIVEN + 2 :]
    held, refs = refs[:GIVEN], refs[GIVEN:]
    (
        span_ref, span_prev_ref, drafts_ref, earlier_ref, ordinal_s, approved_s, _, _,
        mu_ref, wk, wv, wn, we_ref, logit_ref, snap, wr, state, bonus_ref, gain_ref,
    ) = held
    restored_s, span_len_s = given[6:8]
    (
    xs, xd, tmp, line, out_slots, in_slots, ord_v, ord_s,
    prods, rt, intra, kh, vv, kv_new, fade, lefts, base_out, base_new,
    lsem, s_send, s_recv, d_send, d_recv, z_send, z_recv, x_send, x_recv, o_send, o_recv, o_sem,
    ) = refs
    req = lax.axis_index("req")
    me = lax.axis_index("head")
    mx, mz = req // NZ, lax.rem(req, NZ)

    def along_z(d):
        return lax.rem(mz + (d % NZ), NZ)

    def along_x(d):
        return lax.rem(mx + d, NX)

    barrier = pltpu.get_barrier_semaphore()
    for d in FIRST:
        pl.semaphore_signal(barrier, inc=1, device_id=(mx * NZ + along_z(d), me), device_id_type=MESH)
    for k in range(1, NH):
        pl.semaphore_signal(barrier, inc=1, device_id=(req, lax.rem(me + k, NH)), device_id_type=MESH)
    for d in XS:
        pl.semaphore_signal(barrier, inc=1, device_id=(along_x(d) * NZ + mz, me), device_id_type=MESH)

    local = [pltpu.make_async_copy(src, dst, lsem.at[i]) for i, (src, dst) in enumerate(zip(given, held)) if src.shape != (1,)]
    for c in local:
        c.start()
    for c in local[:2]:
        c.wait()
    mine = pl.ds(pl.multiple_of(me * KS, KS), KS)
    prev8 = jnp.broadcast_to(span_prev_ref[...].astype(F32), (8, KS))
    xs[:, mine] = jnp.concatenate([prev8, span_ref[0].astype(F32)], axis=0).astype(BF16)

    pl.semaphore_wait(barrier, NH - 1 + len(FIRST) + len(XS))

    def spread(buf, send, recv, k, slot):
        ref = buf.at[:, pl.ds(pl.multiple_of(slot * KS, KS), KS)]
        return pltpu.make_async_remote_copy(
            src_ref=ref, dst_ref=ref, send_sem=send.at[k - 1], recv_sem=recv.at[k - 1],
            device_id=(req, lax.rem(me + k, NH)), device_id_type=MESH,
        )

    def tell(i, source):
        ref = ord_v.at[source]
        return pltpu.make_async_remote_copy(
            src_ref=ref, dst_ref=ref, send_sem=o_send.at[i], recv_sem=o_recv.at[i],
            device_id=(along_x(XS[i]) * NZ + mz, me), device_id_type=MESH,
        )

    order = (4, 5, 3, 2, 6, 7, 1)
    for k in order:
        spread(xs, s_send, s_recv, k, me).start()
    for c in local[2:6]:
        c.wait()
    for q in range(Q):
        tmp[0, pl.ds(q * T, T)] = drafts_ref[q, :, :C].astype(F32)
        tmp[1, pl.ds(q * T, T)] = drafts_ref[q, :, C:].astype(F32)
    turned = [jnp.concatenate([tmp[i, pl.ds(t, Q, stride=T)] for t in range(T)], axis=0) for i in range(2)]
    early = earlier_ref[...].astype(F32)
    xd[:, mine] = jnp.concatenate([early, jnp.concatenate(turned, axis=1)], axis=0).astype(BF16)
    sub = lax.broadcasted_iota(jnp.int32, (Q, C), 0)
    accepted = jnp.zeros((Q, C), jnp.int32)
    ordinals = jnp.zeros((Q, C), jnp.int32)
    for q in range(Q):
        accepted = jnp.where(sub == q, approved_s[q], accepted)
        ordinals = jnp.where(sub == q, ordinal_s[q], ordinals)
    ord_v[mx] = ordinals
    for i in range(len(XS)):
        tell(i, mx).start()
    for c in local[6:]:
        c.wait()
    mu = mu_ref[...]
    we = we_ref[...]
    logit = logit_ref[...]

    for k in order:
        spread(xs, s_send, s_recv, k, lax.rem(me + NH - k, NH)).wait_recv()
    for k in order:
        spread(xd, d_send, d_recv, k, me).start()
    both = xs[...].astype(F32)
    blend = mixes(both[8:], pltpu.roll(both, 1, axis=0)[8:], mu)
    key = dot(blend(1), wk[...])
    value = dot(blend(2), wv[...])
    decay = decay_of(blend(3), wn[...], we, logit)
    row = lax.broadcasted_iota(jnp.int32, (SPAN, C), 0)
    valid = row < span_len_s[0]
    key = jnp.where(valid, key, 0.0)
    tail = jnp.where(valid, decay, 1.0)
    for d in (1, 2, 4, 8, 16):
        tail = tail * jnp.where(row < SPAN - d, pltpu.roll(tail, SPAN - d, axis=0), 1.0)
    after = jnp.where(row < SPAN - 1, pltpu.roll(tail, SPAN - 1, axis=0), 1.0)
    whole = jnp.transpose(jnp.broadcast_to(tail[0:1], (8, C)))

    def column(m, q):
        return halves(jnp.broadcast_to(m[:, q : q + 1], (C, C)))

    def beside(ref_pair):
        return jnp.concatenate([ref_pair[0], ref_pair[1]], axis=1)

    rebuilt = column(whole, 0) * beside(snap[0]) + halves(outer3(key * after, value))
    line[slot(0), pl.ds(0, HD)] = rebuilt.astype(BF16)
    place = (restored_s[0] - req * Q).astype(F32)
    line[slot(0), pl.ds(HD, ROWS - HD)] = jnp.full((ROWS - HD, C), place, F32).astype(BF16)

    def hop(i, origin, d, sem):
        return pltpu.make_async_remote_copy(
            src_ref=line.at[slot(origin)], dst_ref=line.at[slot(origin - d)],
            send_sem=z_send.at[i], recv_sem=sem,
            device_id=(mx * NZ + along_z(d), me), device_id_type=MESH,
        )

    def cross(i, source):
        return pltpu.make_async_remote_copy(
            src_ref=out_slots.at[i], dst_ref=in_slots.at[source], send_sem=x_send.at[i], recv_sem=x_recv.at[i],
            device_id=(along_x(XS[i]) * NZ + mz, me), device_id_type=MESH,
        )

    def land(i, rel):
        ref = line.at[slot(rel)]
        pltpu.make_async_remote_copy(
            src_ref=ref, dst_ref=ref, send_sem=z_send.at[i], recv_sem=z_recv.at[i],
            device_id=(mx * NZ + along_z(1), me), device_id_type=MESH,
        ).wait_recv()

    n1, n2 = len(FIRST), len(SECOND)
    moves = [hop(i, 0, d, z_recv.at[i]) for i, d in enumerate(FIRST)]
    for c in moves:
        c.start()
    for i in range(2):
        land(i, -FIRST[i])
    second = [hop(n1 + i, o, d, z_recv.at[n1 + i]) for i, (o, d) in enumerate(SECOND)]
    for c in second:
        c.start()
    for k in order:
        spread(xd, d_send, d_recv, k, lax.rem(me + NH - k, NH)).wait_recv()
    both = xd[...].astype(F32)
    blend = mixes(both[Q:], both[:-Q], mu)
    w = decay_of(blend(3), wn[...], we, logit).reshape(T, Q, C)
    k = dot(blend(1), wk[...]).reshape(T, Q, C)

    v = dot(blend(2), wv[...]).reshape(T, Q, C)
    r = dot(blend(0), wr[...]).reshape(T, Q, C)

    for i in range(len(XS)):
        tell(i, along_x(NX - XS[i])).wait_recv()
    read = pltpu.make_async_copy(ord_v, ord_s, o_sem)
    read.start()
    read.wait()

    prods[pl.ds(0, T)] = r * bonus_ref[...].reshape(1, 1, C) * k
    run = r[1:]
    rt[pl.ds(0, Q)] = r[0]
    base = T
    bases = [0]
    for d in range(1, T):
        bases.append(base)
        prods[pl.ds(base, T - d)] = run * k[: T - d]
        base += T - d
        run = run * w[: T - d]
        rt[pl.ds(d * Q, Q)] = run[0]
        run = run[1:]
    lane_r = lax.broadcasted_iota(jnp.int32, (C, C), 0)
    lane_c = lax.broadcasted_iota(jnp.int32, (C, C), 1)
    ones = jnp.where((lane_r < HD) == (lane_c < HD), 1.0, 0.0).astype(BF16)
    ph, plo = split(prods[...].reshape(base * Q, C))
    scores = (dot(ph, ones) + dot(plo, ones)).reshape(base, Q, C)
    out = scores[0:T] * v
    acc = [out[t] for t in range(T)]
    for d in range(1, T):
        part = scores[bases[d] : bases[d] + T - d] * v[: T - d]
        for t in range(d, T):
            acc[t] = acc[t] + part[t - d]
    for t in range(T):
        intra[pl.ds(t * Q, Q)] = acc[t]

    for i in range(2, n1):
        land(i, -FIRST[i])
    for i in range(n2):
        land(n1 + i, SECOND[i][0] - SECOND[i][1])

    def pack(store, ordinal_of):
        flags = []
        for q in range(Q):
            block = line[lax.rem(ordinal_of(q) // Q + (NZ + R) - mz, NZ)]
            store[pl.ds(q * HD, HD)] = block[:HD]
            flags.append(block[HD : HD + 1].astype(F32))
        store[pl.ds(Q * HD, 8)] = jnp.concatenate(flags, axis=0).astype(BF16)

    for i in range(len(XS)):
        pack(out_slots.at[i], lambda q: ord_s[along_x(XS[i]), q, 0])
        cross(i, mx).start()
    pack(in_slots.at[mx], lambda q: ordinal_s[q])

    tail = jnp.ones((Q, C), F32)
    for t in range(T - 1, -1, -1):
        live = accepted > t
        kh[pl.ds(t * Q, Q)] = jnp.where(live, k[t], 0.0) * tail
        vv[pl.ds(t * Q, Q)] = v[t]
        tail = jnp.where(live, w[t], 1.0) * tail
    whole = jnp.transpose(tail)
    lane16 = lax.broadcasted_iota(jnp.int32, (T, C), 1)

    def pick(res):
        both = res[: 2 * T] + res[2 * T :]
        return jnp.where(lane16 < HD, both[:T], both[T:])

    for q in range(Q):
        mine_q = pl.ds(q, T, stride=Q)
        kv = halves(outer3(kh[mine_q], vv[mine_q]))
        col = column(whole, q)
        start = beside(state[q])
        kv_new[q] = kv
        fade[q] = col
        base_new[q] = col * start + kv
        rq = rt[mine_q]
        lh, ll = split(jnp.concatenate([rq[:, :HD], rq[:, HD:]], axis=0))
        left = jnp.concatenate([lh, ll], axis=0)
        lefts[q] = left
        sh, sl = split(start)
        zero = jnp.zeros((2 * T, C), F32)
        res = dot(left, sh) + jnp.concatenate([dot(lh, sl), zero], axis=0)
        base_out[q] = pick(res)
    for i in range(len(XS)):
        cross(i, along_x(NX - XS[i])).wait_recv()

    outs = []
    for q in range(Q):
        entry = ordinal_s[q] // Q
        source = entry // NZ
        body = in_slots[source, pl.ds(q * HD, HD)]
        flag = in_slots[source, pl.ds(Q * HD, 8)].astype(F32)[q : q + 1]
        hit = flag == (ordinal_s[q] - entry * Q).astype(F32)
        new = jnp.where(hit, fade[q] * body.astype(F32) + kv_new[q], base_new[q])
        new_ref[q, 0] = new[:, :HD]
        new_ref[q, 1] = new[:, HD:]
        res = pick(dot(lefts[q], body))
        outs.append(intra[pl.ds(q, T, stride=Q)] + jnp.where(hit, res, base_out[q]))
    full = jnp.concatenate(outs, axis=0)

    def head_mean(x):
        h, lo = split(x)
        return (dot(h, ones) + dot(lo, ones)) * (1.0 / HD)

    centre = full - head_mean(full)
    normed = centre * lax.rsqrt(head_mean(centre * centre) + NORM_EPS) * gain_ref[...]
    verified_ref[...] = normed.reshape(Q, T, C).astype(BF16)

    for k in order:
        spread(xs, s_send, s_recv, k, me).wait_send()
        spread(xd, d_send, d_recv, k, me).wait_send()
    for c in moves + second:
        c.wait_send()
    for i in range(len(XS)):
        tell(i, mx).wait_send()
        cross(i, mx).wait_send()


def per_device(
    drafts, earlier, state, approved, ordinals, restored, span_len, snap, span, span_prev,
    wr, wk, wv, mu, wn, we, logit, bonus, gain,
):
    given = [
        span, span_prev, drafts, earlier, ordinals, approved, restored, span_len,
        mu, wk, wv, wn.T, we, logit.reshape(1, C), snap, wr, state, bonus.reshape(1, C), gain.reshape(1, C),
    ]
    given = [x if x.size == 1 else pltpu.with_memory_space_constraint(x, pltpu.HBM) for x in given]
    held = [pltpu.SMEM(x.shape, x.dtype) if x.dtype == jnp.int32 else pltpu.VMEM(x.shape, x.dtype) for x in given]
    vmem = pl.BlockSpec(memory_space=pltpu.VMEM)
    dma = pltpu.SemaphoreType.DMA
    pairs = T * (T + 1) // 2
    return pl.pallas_call(
        kernel,
        out_shape=(
            jax.ShapeDtypeStruct((Q, T, C), BF16),
            jax.ShapeDtypeStruct((Q, 2, HD, HD), F32),
        ),
        in_specs=[pl.BlockSpec(memory_space=pltpu.SMEM if x.size == 1 else pltpu.HBM) for x in given],
        out_specs=(vmem, vmem),
        scratch_shapes=held
        + [
            pltpu.VMEM((8 + SPAN, W), BF16),
            pltpu.VMEM((Q + Q * T, W), BF16),
            pltpu.VMEM((2, Q * T, C), F32),
            pltpu.VMEM((NZ, ROWS, C), BF16),
            pltpu.VMEM((len(XS), PACK, C), BF16),
            pltpu.VMEM((NX, PACK, C), BF16),
            pltpu.VMEM((NX, Q, C), jnp.int32),
            pltpu.SMEM((NX, Q, C), jnp.int32),
            pltpu.VMEM((pairs, Q, C), F32),
            pltpu.VMEM((T * Q, C), F32),
            pltpu.VMEM((T * Q, C), F32),
            pltpu.VMEM((T * Q, C), F32),
            pltpu.VMEM((T * Q, C), F32),
            pltpu.VMEM((Q, HD, C), F32),
            pltpu.VMEM((Q, HD, C), F32),
            pltpu.VMEM((Q, 4 * T, HD), BF16),
            pltpu.VMEM((Q, T, C), F32),
            pltpu.VMEM((Q, HD, C), F32),
            dma((GIVEN,)), dma((NH - 1,)), dma((NH - 1,)), dma((NH - 1,)), dma((NH - 1,)),
            dma((NZ - 1,)), dma((NZ - 1,)), dma((len(XS),)), dma((len(XS),)), dma((len(XS),)), dma((len(XS),)), dma,
        ],
        compiler_params=pltpu.CompilerParams(
            collective_id=0, has_side_effects=True, vmem_limit_bytes=32 * 1024 * 1024
        ),
    )(*given)


def solution(mesh):
    in_specs = (
        P("req", None, "head"), P("req", "head"), P("req", "head", None, None), P("req"), P("req"), P("req"), P("req"),
        P("req", "head", None, None), P("req", None, "head"), P("req", "head"), P(None, "head"), P(None, "head"),
        P(None, "head"), P(), P(), P(None, "head"), P("head"), P("head"), P("head"),
    )
    out_specs = (P("req", None, "head"), P("req", "head", None, None))
    return jax.shard_map(per_device, mesh=mesh, in_specs=in_specs, out_specs=out_specs, check_vma=False)
```

```python
import jax
import jax.numpy as jnp
from jax import lax
from jax.experimental import pallas as pl
from jax.experimental.pallas import tpu as pltpu
from jax.sharding import PartitionSpec as P

MESH = pl.DeviceIdType.MESH
F32 = jnp.float32
BF16 = jnp.bfloat16

NX, NZ, NH = 4, 16, 8
T = 16
SPAN = 32
Q = 8
W = 2048
KS = W // NH
C = 128
HD = 64
ROWS = 72
NORM_EPS = 0.00064


GIVEN = 19
R = 4
FIRST = tuple(d for i in range(R, 0, -1) for d in (i, -i))
SECOND = tuple((-R, d) for d in range(8 - R, 0, -1)) + tuple((R, -d) for d in range(7 - R, 0, -1))
XS = (2, 1, 3)


PACK = Q * HD + 8


def slot(rel):
    return (rel + R) % NZ


def split(x):
    hi = x.astype(BF16)
    return hi, (x - hi.astype(F32)).astype(BF16)


def dot(a, b):
    return jnp.dot(a, b, preferred_element_type=F32)


def dot_t(a, b):
    return lax.dot_general(a, b, (((0,), (0,)), ((), ())), preferred_element_type=F32)


def outer3(a, b):
    ah, al = split(a)
    bh, bl = split(b)
    return dot_t(ah, bh) + dot_t(ah, bl) + dot_t(al, bh)


def halves(m):
    lane = lax.broadcasted_iota(jnp.int32, (HD, C), 1)
    return jnp.where(lane < HD, m[:HD], m[HD:])


def mixes(cur, prev, mu):
    change = prev - cur
    return lambda m: (cur + change * mu[m : m + 1]).astype(BF16)


def decay_of(low, wn, we, logit):
    low_rank = lax.dot_general(low, wn, (((1,), (1,)), ((), ())), preferred_element_type=F32)
    rank = jnp.tanh(low_rank).astype(BF16)
    return jnp.exp(-jnp.exp(logit + dot(rank, we)))


def kernel(*refs):
    given, (verified_ref, new_ref), refs = refs[:GIVEN], refs[GIVEN : GIVEN + 2], refs[GIVEN + 2 :]
    held, refs = refs[:GIVEN], refs[GIVEN:]
    (
        span_ref, span_prev_ref, drafts_ref, earlier_ref, ordinal_s, approved_s, _, _,
        mu_ref, wk, wv, wn, we_ref, logit_ref, snap, wr, state, bonus_ref, gain_ref,
    ) = held
    restored_s, span_len_s = given[6:8]
    (
    xs, xd, tmp, line, out_slots, in_slots, ord_v, ord_s,
    prods, rt, intra, kh, vv, kv_new, fade, lefts, base_out, base_new,
    lsem, s_send, s_recv, d_send, d_recv, z_send, z_recv, x_send, x_recv, o_send, o_recv, o_sem, near_sem, far_sem,
    ) = refs
    req = lax.axis_index("req")
    me = lax.axis_index("head")
    mx, mz = req // NZ, lax.rem(req, NZ)

    def along_z(d):
        return lax.rem(mz + (d % NZ), NZ)

    def along_x(d):
        return lax.rem(mx + d, NX)

    barrier = pltpu.get_barrier_semaphore()
    for d in (1, -1):
        pl.semaphore_signal(barrier, inc=1, device_id=(mx * NZ + along_z(d), me), device_id_type=MESH)
    for k in range(1, NH):
        pl.semaphore_signal(barrier, inc=1, device_id=(req, lax.rem(me + k, NH)), device_id_type=MESH)
    for d in XS:
        pl.semaphore_signal(barrier, inc=1, device_id=(along_x(d) * NZ + mz, me), device_id_type=MESH)

    local = [pltpu.make_async_copy(src, dst, lsem.at[i]) for i, (src, dst) in enumerate(zip(given, held)) if src.shape != (1,)]
    for c in local:
        c.start()
    for c in local[:2]:
        c.wait()
    mine = pl.ds(pl.multiple_of(me * KS, KS), KS)
    prev8 = jnp.broadcast_to(span_prev_ref[...].astype(F32), (8, KS))
    xs[:, mine] = jnp.concatenate([prev8, span_ref[0].astype(F32)], axis=0).astype(BF16)

    def vouch(reach, sem):
        for d in (reach, -reach):
            pl.semaphore_signal(sem, inc=1, device_id=(mx * NZ + along_z(d), me), device_id_type=MESH)

    pl.semaphore_wait(barrier, NH - 1 + 2 + len(XS))

    def spread(buf, send, recv, k, slot):
        ref = buf.at[:, pl.ds(pl.multiple_of(slot * KS, KS), KS)]
        return pltpu.make_async_remote_copy(
            src_ref=ref, dst_ref=ref, send_sem=send.at[k - 1], recv_sem=recv.at[k - 1],
            device_id=(req, lax.rem(me + k, NH)), device_id_type=MESH,
        )

    def tell(i, source):
        ref = ord_v.at[source]
        return pltpu.make_async_remote_copy(
            src_ref=ref, dst_ref=ref, send_sem=o_send.at[i], recv_sem=o_recv.at[i],
            device_id=(along_x(XS[i]) * NZ + mz, me), device_id_type=MESH,
        )

    order = (4, 5, 3, 2, 6, 7, 1)
    for k in order:
        spread(xs, s_send, s_recv, k, me).start()
    vouch(1, near_sem)
    for c in local[2:6]:
        c.wait()
    for q in range(Q):
        tmp[0, pl.ds(q * T, T)] = drafts_ref[q, :, :C].astype(F32)
        tmp[1, pl.ds(q * T, T)] = drafts_ref[q, :, C:].astype(F32)
    turned = [jnp.concatenate([tmp[i, pl.ds(t, Q, stride=T)] for t in range(T)], axis=0) for i in range(2)]
    early = earlier_ref[...].astype(F32)
    xd[:, mine] = jnp.concatenate([early, jnp.concatenate(turned, axis=1)], axis=0).astype(BF16)
    sub = lax.broadcasted_iota(jnp.int32, (Q, C), 0)
    accepted = jnp.zeros((Q, C), jnp.int32)
    ordinals = jnp.zeros((Q, C), jnp.int32)
    for q in range(Q):
        accepted = jnp.where(sub == q, approved_s[q], accepted)
        ordinals = jnp.where(sub == q, ordinal_s[q], ordinals)
    ord_v[mx] = ordinals
    for i in range(len(XS)):
        tell(i, mx).start()
    pl.semaphore_wait(near_sem, 2)
    vouch(2, far_sem)
    for c in local[6:]:
        c.wait()
    mu = mu_ref[...]
    we = we_ref[...]
    logit = logit_ref[...]

    for k in order:
        spread(xs, s_send, s_recv, k, lax.rem(me + NH - k, NH)).wait_recv()
    for k in order:
        spread(xd, d_send, d_recv, k, me).start()
    both = xs[...].astype(F32)
    blend = mixes(both[8:], pltpu.roll(both, 1, axis=0)[8:], mu)
    key = dot(blend(1), wk[...])
    value = dot(blend(2), wv[...])
    decay = decay_of(blend(3), wn[...], we, logit)
    row = lax.broadcasted_iota(jnp.int32, (SPAN, C), 0)
    valid = row < span_len_s[0]
    key = jnp.where(valid, key, 0.0)
    tail = jnp.where(valid, decay, 1.0)
    for d in (1, 2, 4, 8, 16):
        tail = tail * jnp.where(row < SPAN - d, pltpu.roll(tail, SPAN - d, axis=0), 1.0)
    after = jnp.where(row < SPAN - 1, pltpu.roll(tail, SPAN - 1, axis=0), 1.0)
    whole = jnp.transpose(jnp.broadcast_to(tail[0:1], (8, C)))

    def column(m, q):
        return halves(jnp.broadcast_to(m[:, q : q + 1], (C, C)))

    def beside(ref_pair):
        return jnp.concatenate([ref_pair[0], ref_pair[1]], axis=1)

    rebuilt = column(whole, 0) * beside(snap[0]) + halves(outer3(key * after, value))
    line[slot(0), pl.ds(0, HD)] = rebuilt.astype(BF16)
    place = (restored_s[0] - req * Q).astype(F32)
    line[slot(0), pl.ds(HD, ROWS - HD)] = jnp.full((ROWS - HD, C), place, F32).astype(BF16)

    def hop(i, origin, d, sem):
        return pltpu.make_async_remote_copy(
            src_ref=line.at[slot(origin)], dst_ref=line.at[slot(origin - d)],
            send_sem=z_send.at[i], recv_sem=sem,
            device_id=(mx * NZ + along_z(d), me), device_id_type=MESH,
        )

    def cross(i, source):
        return pltpu.make_async_remote_copy(
            src_ref=out_slots.at[i], dst_ref=in_slots.at[source], send_sem=x_send.at[i], recv_sem=x_recv.at[i],
            device_id=(along_x(XS[i]) * NZ + mz, me), device_id_type=MESH,
        )

    def land(i, rel):
        ref = line.at[slot(rel)]
        pltpu.make_async_remote_copy(
            src_ref=ref, dst_ref=ref, send_sem=z_send.at[i], recv_sem=z_recv.at[i],
            device_id=(mx * NZ + along_z(1), me), device_id_type=MESH,
        ).wait_recv()

    n1, n2 = len(FIRST), len(SECOND)
    pl.semaphore_wait(far_sem, 2)
    moves = [hop(i, 0, d, z_recv.at[i]) for i, d in enumerate(FIRST)]
    for c in moves:
        c.start()
    for i in range(2):
        land(i, -FIRST[i])
    second = [hop(n1 + i, o, d, z_recv.at[n1 + i]) for i, (o, d) in enumerate(SECOND)]
    for c in second:
        c.start()
    for i in range(len(XS)):
        tell(i, along_x(NX - XS[i])).wait_recv()
    read = pltpu.make_async_copy(ord_v, ord_s, o_sem)
    read.start()
    read.wait()

    for i in range(2, n1):
        land(i, -FIRST[i])
    for i in range(n2):
        land(n1 + i, SECOND[i][0] - SECOND[i][1])

    def pack(store, ordinal_of):
        flags = []
        for q in range(Q):
            block = line[lax.rem(ordinal_of(q) // Q + (NZ + R) - mz, NZ)]
            store[pl.ds(q * HD, HD)] = block[:HD]
            flags.append(block[HD : HD + 1].astype(F32))
        store[pl.ds(Q * HD, 8)] = jnp.concatenate(flags, axis=0).astype(BF16)

    for i in range(len(XS)):
        pack(out_slots.at[i], lambda q: ord_s[along_x(XS[i]), q, 0])
        cross(i, mx).start()
    pack(in_slots.at[mx], lambda q: ordinal_s[q])

    for k in order:
        spread(xd, d_send, d_recv, k, lax.rem(me + NH - k, NH)).wait_recv()
    both = xd[...].astype(F32)
    blend = mixes(both[Q:], both[:-Q], mu)
    w = decay_of(blend(3), wn[...], we, logit).reshape(T, Q, C)
    k = dot(blend(1), wk[...]).reshape(T, Q, C)

    v = dot(blend(2), wv[...]).reshape(T, Q, C)
    r = dot(blend(0), wr[...]).reshape(T, Q, C)

    prods[pl.ds(0, T)] = r * bonus_ref[...].reshape(1, 1, C) * k
    run = r[1:]
    rt[pl.ds(0, Q)] = r[0]
    base = T
    bases = [0]
    for d in range(1, T):
        bases.append(base)
        prods[pl.ds(base, T - d)] = run * k[: T - d]
        base += T - d
        run = run * w[: T - d]
        rt[pl.ds(d * Q, Q)] = run[0]
        run = run[1:]
    lane_r = lax.broadcasted_iota(jnp.int32, (C, C), 0)
    lane_c = lax.broadcasted_iota(jnp.int32, (C, C), 1)
    ones = jnp.where((lane_r < HD) == (lane_c < HD), 1.0, 0.0).astype(BF16)
    ph, plo = split(prods[...].reshape(base * Q, C))
    scores = (dot(ph, ones) + dot(plo, ones)).reshape(base, Q, C)
    out = scores[0:T] * v
    acc = [out[t] for t in range(T)]
    for d in range(1, T):
        part = scores[bases[d] : bases[d] + T - d] * v[: T - d]
        for t in range(d, T):
            acc[t] = acc[t] + part[t - d]
    for t in range(T):
        intra[pl.ds(t * Q, Q)] = acc[t]

    tail = jnp.ones((Q, C), F32)
    for t in range(T - 1, -1, -1):
        live = accepted > t
        kh[pl.ds(t * Q, Q)] = jnp.where(live, k[t], 0.0) * tail
        vv[pl.ds(t * Q, Q)] = v[t]
        tail = jnp.where(live, w[t], 1.0) * tail
    whole = jnp.transpose(tail)
    lane16 = lax.broadcasted_iota(jnp.int32, (T, C), 1)

    def pick(res):
        both = res[: 2 * T] + res[2 * T :]
        return jnp.where(lane16 < HD, both[:T], both[T:])

    for q in range(Q):
        mine_q = pl.ds(q, T, stride=Q)
        kv = halves(outer3(kh[mine_q], vv[mine_q]))
        col = column(whole, q)
        start = beside(state[q])
        kv_new[q] = kv
        fade[q] = col
        base_new[q] = col * start + kv
        rq = rt[mine_q]
        lh, ll = split(jnp.concatenate([rq[:, :HD], rq[:, HD:]], axis=0))
        left = jnp.concatenate([lh, ll], axis=0)
        lefts[q] = left
        sh, sl = split(start)
        zero = jnp.zeros((2 * T, C), F32)
        res = dot(left, sh) + jnp.concatenate([dot(lh, sl), zero], axis=0)
        base_out[q] = pick(res)
    for i in range(len(XS)):
        cross(i, along_x(NX - XS[i])).wait_recv()

    outs = []
    for q in range(Q):
        entry = ordinal_s[q] // Q
        source = entry // NZ
        body = in_slots[source, pl.ds(q * HD, HD)]
        flag = in_slots[source, pl.ds(Q * HD, 8)].astype(F32)[q : q + 1]
        hit = flag == (ordinal_s[q] - entry * Q).astype(F32)
        new = jnp.where(hit, fade[q] * body.astype(F32) + kv_new[q], base_new[q])
        new_ref[q, 0] = new[:, :HD]
        new_ref[q, 1] = new[:, HD:]
        res = pick(dot(lefts[q], body))
        outs.append(intra[pl.ds(q, T, stride=Q)] + jnp.where(hit, res, base_out[q]))
    full = jnp.concatenate(outs, axis=0)

    def head_mean(x):
        h, lo = split(x)
        return (dot(h, ones) + dot(lo, ones)) * (1.0 / HD)

    centre = full - head_mean(full)
    normed = centre * lax.rsqrt(head_mean(centre * centre) + NORM_EPS) * gain_ref[...]
    verified_ref[...] = normed.reshape(Q, T, C).astype(BF16)

    for k in order:
        spread(xs, s_send, s_recv, k, me).wait_send()
        spread(xd, d_send, d_recv, k, me).wait_send()
    for c in moves + second:
        c.wait_send()
    for i in range(len(XS)):
        tell(i, mx).wait_send()
        cross(i, mx).wait_send()


def per_device(
    drafts, earlier, state, approved, ordinals, restored, span_len, snap, span, span_prev,
    wr, wk, wv, mu, wn, we, logit, bonus, gain,
):
    given = [
        span, span_prev, drafts, earlier, ordinals, approved, restored, span_len,
        mu, wk, wv, wn.T, we, logit.reshape(1, C), snap, wr, state, bonus.reshape(1, C), gain.reshape(1, C),
    ]
    given = [x if x.size == 1 else pltpu.with_memory_space_constraint(x, pltpu.HBM) for x in given]
    held = [pltpu.SMEM(x.shape, x.dtype) if x.dtype == jnp.int32 else pltpu.VMEM(x.shape, x.dtype) for x in given]
    vmem = pl.BlockSpec(memory_space=pltpu.VMEM)
    dma = pltpu.SemaphoreType.DMA
    pairs = T * (T + 1) // 2
    return pl.pallas_call(
        kernel,
        out_shape=(
            jax.ShapeDtypeStruct((Q, T, C), BF16),
            jax.ShapeDtypeStruct((Q, 2, HD, HD), F32),
        ),
        in_specs=[pl.BlockSpec(memory_space=pltpu.SMEM if x.size == 1 else pltpu.HBM) for x in given],
        out_specs=(vmem, vmem),
        scratch_shapes=held
        + [
            pltpu.VMEM((8 + SPAN, W), BF16),
            pltpu.VMEM((Q + Q * T, W), BF16),
            pltpu.VMEM((2, Q * T, C), F32),
            pltpu.VMEM((NZ, ROWS, C), BF16),
            pltpu.VMEM((len(XS), PACK, C), BF16),
            pltpu.VMEM((NX, PACK, C), BF16),
            pltpu.VMEM((NX, Q, C), jnp.int32),
            pltpu.SMEM((NX, Q, C), jnp.int32),
            pltpu.VMEM((pairs, Q, C), F32),
            pltpu.VMEM((T * Q, C), F32),
            pltpu.VMEM((T * Q, C), F32),
            pltpu.VMEM((T * Q, C), F32),
            pltpu.VMEM((T * Q, C), F32),
            pltpu.VMEM((Q, HD, C), F32),
            pltpu.VMEM((Q, HD, C), F32),
            pltpu.VMEM((Q, 4 * T, HD), BF16),
            pltpu.VMEM((Q, T, C), F32),
            pltpu.VMEM((Q, HD, C), F32),
            dma((GIVEN,)), dma((NH - 1,)), dma((NH - 1,)), dma((NH - 1,)), dma((NH - 1,)),
            dma((NZ - 1,)), dma((NZ - 1,)), dma((len(XS),)), dma((len(XS),)), dma((len(XS),)), dma((len(XS),)), dma,
            pltpu.SemaphoreType.REGULAR, pltpu.SemaphoreType.REGULAR,
        ],
        compiler_params=pltpu.CompilerParams(
            collective_id=0, has_side_effects=True, vmem_limit_bytes=32 * 1024 * 1024
        ),
    )(*given)


def solution(mesh):
    in_specs = (
        P("req", None, "head"), P("req", "head"), P("req", "head", None, None), P("req"), P("req"), P("req"), P("req"),
        P("req", "head", None, None), P("req", None, "head"), P("req", "head"), P(None, "head"), P(None, "head"),
        P(None, "head"), P(), P(), P(None, "head"), P("head"), P("head"), P("head"),
    )
    out_specs = (P("req", None, "head"), P("req", "head", None, None))
    return jax.shard_map(per_device, mesh=mesh, in_specs=in_specs, out_specs=out_specs, check_vma=False)
```

```python
import jax
import jax.numpy as jnp
from jax import lax
from jax.experimental import pallas as pl
from jax.experimental.pallas import tpu as pltpu
from jax.sharding import PartitionSpec as P

MESH = pl.DeviceIdType.MESH
F32 = jnp.float32
BF16 = jnp.bfloat16

NX, NZ, NH = 4, 16, 8
T = 16
SPAN = 32
Q = 8
W = 2048
KS = W // NH
C = 128
HD = 64
ROWS = 72
NORM_EPS = 0.00064


GIVEN = 19
R = 4
FIRST = tuple(d for i in range(R, 0, -1) for d in (i, -i))
SECOND = ((-4, 4), (4, -4), (-4, 3), (4, -3), (-4, 2), (4, -2), (-4, 1), (4, -1))
SHARE = {(-4, 4): (0, 32), (4, -4): (32, 40)}
XS = (2, 1, 3)


PACK = Q * HD + 8


def slot(rel):
    return (rel + R) % NZ


def split(x):
    hi = x.astype(BF16)
    return hi, (x - hi.astype(F32)).astype(BF16)


def dot(a, b):
    return jnp.dot(a, b, preferred_element_type=F32)


def dot_t(a, b):
    return lax.dot_general(a, b, (((0,), (0,)), ((), ())), preferred_element_type=F32)


def outer3(a, b):
    ah, al = split(a)
    bh, bl = split(b)
    return dot_t(ah, bh) + dot_t(ah, bl) + dot_t(al, bh)


def halves(m):
    lane = lax.broadcasted_iota(jnp.int32, (HD, C), 1)
    return jnp.where(lane < HD, m[:HD], m[HD:])


def mixes(cur, prev, mu):
    change = prev - cur
    return lambda m: (cur + change * mu[m : m + 1]).astype(BF16)


def decay_of(low, wn, we, logit):
    low_rank = lax.dot_general(low, wn, (((1,), (1,)), ((), ())), preferred_element_type=F32)
    rank = jnp.tanh(low_rank).astype(BF16)
    return jnp.exp(-jnp.exp(logit + dot(rank, we)))


def kernel(*refs):
    given, (verified_ref, new_ref), refs = refs[:GIVEN], refs[GIVEN : GIVEN + 2], refs[GIVEN + 2 :]
    held, refs = refs[:GIVEN], refs[GIVEN:]
    (
        span_ref, span_prev_ref, drafts_ref, earlier_ref, ordinal_s, approved_s, _, _,
        mu_ref, wk, wv, wn, we_ref, logit_ref, snap, wr, state, bonus_ref, gain_ref,
    ) = held
    restored_s, span_len_s = given[6:8]
    (
    xs, xd, tmp, line, out_slots, in_slots, ord_v, ord_s,
    prods, rt, intra, kh, vv, kv_new, fade, lefts, base_out, base_new,
    lsem, s_send, s_recv, d_send, d_recv, z_send, z_recv, x_send, x_recv, o_send, o_recv, o_sem, near_sem, far_sem,
    ) = refs
    req = lax.axis_index("req")
    me = lax.axis_index("head")
    mx, mz = req // NZ, lax.rem(req, NZ)

    def along_z(d):
        return lax.rem(mz + (d % NZ), NZ)

    def along_x(d):
        return lax.rem(mx + d, NX)

    barrier = pltpu.get_barrier_semaphore()
    for d in (1, -1):
        pl.semaphore_signal(barrier, inc=1, device_id=(mx * NZ + along_z(d), me), device_id_type=MESH)
    for k in range(1, NH):
        pl.semaphore_signal(barrier, inc=1, device_id=(req, lax.rem(me + k, NH)), device_id_type=MESH)
    for d in XS:
        pl.semaphore_signal(barrier, inc=1, device_id=(along_x(d) * NZ + mz, me), device_id_type=MESH)

    local = [pltpu.make_async_copy(src, dst, lsem.at[i]) for i, (src, dst) in enumerate(zip(given, held)) if src.shape != (1,)]
    for c in local:
        c.start()
    for c in local[:2]:
        c.wait()
    mine = pl.ds(pl.multiple_of(me * KS, KS), KS)
    prev8 = jnp.broadcast_to(span_prev_ref[...].astype(F32), (8, KS))
    xs[:, mine] = jnp.concatenate([prev8, span_ref[0].astype(F32)], axis=0).astype(BF16)

    def vouch(reach, sem):
        for d in (reach, -reach):
            pl.semaphore_signal(sem, inc=1, device_id=(mx * NZ + along_z(d), me), device_id_type=MESH)

    pl.semaphore_wait(barrier, NH - 1 + 2 + len(XS))

    def spread(buf, send, recv, k, slot):
        ref = buf.at[:, pl.ds(pl.multiple_of(slot * KS, KS), KS)]
        return pltpu.make_async_remote_copy(
            src_ref=ref, dst_ref=ref, send_sem=send.at[k - 1], recv_sem=recv.at[k - 1],
            device_id=(req, lax.rem(me + k, NH)), device_id_type=MESH,
        )

    def tell(i, source):
        ref = ord_v.at[source]
        return pltpu.make_async_remote_copy(
            src_ref=ref, dst_ref=ref, send_sem=o_send.at[i], recv_sem=o_recv.at[i],
            device_id=(along_x(XS[i]) * NZ + mz, me), device_id_type=MESH,
        )

    order = (4, 5, 3, 2, 6, 7, 1)
    for k in order:
        spread(xs, s_send, s_recv, k, me).start()
    vouch(1, near_sem)
    for c in local[2:6]:
        c.wait()
    for q in range(Q):
        tmp[0, pl.ds(q * T, T)] = drafts_ref[q, :, :C].astype(F32)
        tmp[1, pl.ds(q * T, T)] = drafts_ref[q, :, C:].astype(F32)
    turned = [jnp.concatenate([tmp[i, pl.ds(t, Q, stride=T)] for t in range(T)], axis=0) for i in range(2)]
    early = earlier_ref[...].astype(F32)
    xd[:, mine] = jnp.concatenate([early, jnp.concatenate(turned, axis=1)], axis=0).astype(BF16)
    sub = lax.broadcasted_iota(jnp.int32, (Q, C), 0)
    accepted = jnp.zeros((Q, C), jnp.int32)
    ordinals = jnp.zeros((Q, C), jnp.int32)
    for q in range(Q):
        accepted = jnp.where(sub == q, approved_s[q], accepted)
        ordinals = jnp.where(sub == q, ordinal_s[q], ordinals)
    ord_v[mx] = ordinals
    for i in range(len(XS)):
        tell(i, mx).start()
    pl.semaphore_wait(near_sem, 2)
    vouch(2, far_sem)
    for c in local[6:]:
        c.wait()
    mu = mu_ref[...]
    we = we_ref[...]
    logit = logit_ref[...]

    for k in order:
        spread(xs, s_send, s_recv, k, lax.rem(me + NH - k, NH)).wait_recv()
    for k in order:
        spread(xd, d_send, d_recv, k, me).start()
    both = xs[...].astype(F32)
    blend = mixes(both[8:], pltpu.roll(both, 1, axis=0)[8:], mu)
    key = dot(blend(1), wk[...])
    value = dot(blend(2), wv[...])
    decay = decay_of(blend(3), wn[...], we, logit)
    row = lax.broadcasted_iota(jnp.int32, (SPAN, C), 0)
    valid = row < span_len_s[0]
    key = jnp.where(valid, key, 0.0)
    tail = jnp.where(valid, decay, 1.0)
    for d in (1, 2, 4, 8, 16):
        tail = tail * jnp.where(row < SPAN - d, pltpu.roll(tail, SPAN - d, axis=0), 1.0)
    after = jnp.where(row < SPAN - 1, pltpu.roll(tail, SPAN - 1, axis=0), 1.0)
    whole = jnp.transpose(jnp.broadcast_to(tail[0:1], (8, C)))

    def column(m, q):
        return halves(jnp.broadcast_to(m[:, q : q + 1], (C, C)))

    def beside(ref_pair):
        return jnp.concatenate([ref_pair[0], ref_pair[1]], axis=1)

    rebuilt = column(whole, 0) * beside(snap[0]) + halves(outer3(key * after, value))
    line[slot(0), pl.ds(0, HD)] = rebuilt.astype(BF16)
    place = (restored_s[0] - req * Q).astype(F32)
    line[slot(0), pl.ds(HD, ROWS - HD)] = jnp.full((ROWS - HD, C), place, F32).astype(BF16)

    def hop(i, origin, d, sem):
        part = pl.ds(*SHARE.get((origin, d), (0, ROWS)))
        return pltpu.make_async_remote_copy(
            src_ref=line.at[slot(origin), part], dst_ref=line.at[slot(origin - d), part],
            send_sem=z_send.at[i], recv_sem=sem,
            device_id=(mx * NZ + along_z(d), me), device_id_type=MESH,
        )

    def cross(i, source):
        return pltpu.make_async_remote_copy(
            src_ref=out_slots.at[i], dst_ref=in_slots.at[source], send_sem=x_send.at[i], recv_sem=x_recv.at[i],
            device_id=(along_x(XS[i]) * NZ + mz, me), device_id_type=MESH,
        )

    def land(i, rel, part=(0, ROWS)):
        ref = line.at[slot(rel), pl.ds(*part)]
        pltpu.make_async_remote_copy(
            src_ref=ref, dst_ref=ref, send_sem=z_send.at[i], recv_sem=z_recv.at[i],
            device_id=(mx * NZ + along_z(1), me), device_id_type=MESH,
        ).wait_recv()

    n1, n2 = len(FIRST), len(SECOND)
    pl.semaphore_wait(far_sem, 2)
    moves = [hop(i, 0, d, z_recv.at[i]) for i, d in enumerate(FIRST)]
    for c in moves:
        c.start()
    for i in range(2):
        land(i, -FIRST[i])
    second = [hop(n1 + i, o, d, z_recv.at[n1 + i]) for i, (o, d) in enumerate(SECOND)]
    for c in second:
        c.start()
    for i in range(len(XS)):
        tell(i, along_x(NX - XS[i])).wait_recv()
    read = pltpu.make_async_copy(ord_v, ord_s, o_sem)
    read.start()
    read.wait()

    for i in range(2, n1):
        land(i, -FIRST[i])
    for i in range(n2):
        land(n1 + i, SECOND[i][0] - SECOND[i][1], SHARE.get(SECOND[i], (0, ROWS)))

    def pack(store, ordinal_of):
        flags = []
        for q in range(Q):
            block = line[lax.rem(ordinal_of(q) // Q + (NZ + R) - mz, NZ)]
            store[pl.ds(q * HD, HD)] = block[:HD]
            flags.append(block[HD : HD + 1].astype(F32))
        store[pl.ds(Q * HD, 8)] = jnp.concatenate(flags, axis=0).astype(BF16)

    for i in range(len(XS)):
        pack(out_slots.at[i], lambda q: ord_s[along_x(XS[i]), q, 0])
        cross(i, mx).start()
    pack(in_slots.at[mx], lambda q: ordinal_s[q])

    for k in order:
        spread(xd, d_send, d_recv, k, lax.rem(me + NH - k, NH)).wait_recv()
    both = xd[...].astype(F32)
    blend = mixes(both[Q:], both[:-Q], mu)
    w = decay_of(blend(3), wn[...], we, logit).reshape(T, Q, C)
    k = dot(blend(1), wk[...]).reshape(T, Q, C)

    v = dot(blend(2), wv[...]).reshape(T, Q, C)
    r = dot(blend(0), wr[...]).reshape(T, Q, C)

    prods[pl.ds(0, T)] = r * bonus_ref[...].reshape(1, 1, C) * k
    run = r[1:]
    rt[pl.ds(0, Q)] = r[0]
    base = T
    bases = [0]
    for d in range(1, T):
        bases.append(base)
        prods[pl.ds(base, T - d)] = run * k[: T - d]
        base += T - d
        run = run * w[: T - d]
        rt[pl.ds(d * Q, Q)] = run[0]
        run = run[1:]
    lane_r = lax.broadcasted_iota(jnp.int32, (C, C), 0)
    lane_c = lax.broadcasted_iota(jnp.int32, (C, C), 1)
    ones = jnp.where((lane_r < HD) == (lane_c < HD), 1.0, 0.0).astype(BF16)
    ph, plo = split(prods[...].reshape(base * Q, C))
    scores = (dot(ph, ones) + dot(plo, ones)).reshape(base, Q, C)
    out = scores[0:T] * v
    acc = [out[t] for t in range(T)]
    for d in range(1, T):
        part = scores[bases[d] : bases[d] + T - d] * v[: T - d]
        for t in range(d, T):
            acc[t] = acc[t] + part[t - d]
    for t in range(T):
        intra[pl.ds(t * Q, Q)] = acc[t]

    tail = jnp.ones((Q, C), F32)
    for t in range(T - 1, -1, -1):
        live = accepted > t
        kh[pl.ds(t * Q, Q)] = jnp.where(live, k[t], 0.0) * tail
        vv[pl.ds(t * Q, Q)] = v[t]
        tail = jnp.where(live, w[t], 1.0) * tail
    whole = jnp.transpose(tail)
    lane16 = lax.broadcasted_iota(jnp.int32, (T, C), 1)

    def pick(res):
        both = res[: 2 * T] + res[2 * T :]
        return jnp.where(lane16 < HD, both[:T], both[T:])

    for q in range(Q):
        mine_q = pl.ds(q, T, stride=Q)
        kv = halves(outer3(kh[mine_q], vv[mine_q]))
        col = column(whole, q)
        start = beside(state[q])
        kv_new[q] = kv
        fade[q] = col
        base_new[q] = col * start + kv
        rq = rt[mine_q]
        lh, ll = split(jnp.concatenate([rq[:, :HD], rq[:, HD:]], axis=0))
        left = jnp.concatenate([lh, ll], axis=0)
        lefts[q] = left
        sh, sl = split(start)
        zero = jnp.zeros((2 * T, C), F32)
        res = dot(left, sh) + jnp.concatenate([dot(lh, sl), zero], axis=0)
        base_out[q] = pick(res)
    for i in range(len(XS)):
        cross(i, along_x(NX - XS[i])).wait_recv()

    outs = []
    for q in range(Q):
        entry = ordinal_s[q] // Q
        source = entry // NZ
        body = in_slots[source, pl.ds(q * HD, HD)]
        flag = in_slots[source, pl.ds(Q * HD, 8)].astype(F32)[q : q + 1]
        hit = flag == (ordinal_s[q] - entry * Q).astype(F32)
        new = jnp.where(hit, fade[q] * body.astype(F32) + kv_new[q], base_new[q])
        new_ref[q, 0] = new[:, :HD]
        new_ref[q, 1] = new[:, HD:]
        res = pick(dot(lefts[q], body))
        outs.append(intra[pl.ds(q, T, stride=Q)] + jnp.where(hit, res, base_out[q]))
    full = jnp.concatenate(outs, axis=0)

    def head_mean(x):
        h, lo = split(x)
        return (dot(h, ones) + dot(lo, ones)) * (1.0 / HD)

    centre = full - head_mean(full)
    normed = centre * lax.rsqrt(head_mean(centre * centre) + NORM_EPS) * gain_ref[...]
    verified_ref[...] = normed.reshape(Q, T, C).astype(BF16)

    for k in order:
        spread(xs, s_send, s_recv, k, me).wait_send()
        spread(xd, d_send, d_recv, k, me).wait_send()
    for c in moves + second:
        c.wait_send()
    for i in range(len(XS)):
        tell(i, mx).wait_send()
        cross(i, mx).wait_send()


def per_device(
    drafts, earlier, state, approved, ordinals, restored, span_len, snap, span, span_prev,
    wr, wk, wv, mu, wn, we, logit, bonus, gain,
):
    given = [
        span, span_prev, drafts, earlier, ordinals, approved, restored, span_len,
        mu, wk, wv, wn.T, we, logit.reshape(1, C), snap, wr, state, bonus.reshape(1, C), gain.reshape(1, C),
    ]
    given = [x if x.size == 1 else pltpu.with_memory_space_constraint(x, pltpu.HBM) for x in given]
    held = [pltpu.SMEM(x.shape, x.dtype) if x.dtype == jnp.int32 else pltpu.VMEM(x.shape, x.dtype) for x in given]
    vmem = pl.BlockSpec(memory_space=pltpu.VMEM)
    dma = pltpu.SemaphoreType.DMA
    pairs = T * (T + 1) // 2
    return pl.pallas_call(
        kernel,
        out_shape=(
            jax.ShapeDtypeStruct((Q, T, C), BF16),
            jax.ShapeDtypeStruct((Q, 2, HD, HD), F32),
        ),
        in_specs=[pl.BlockSpec(memory_space=pltpu.SMEM if x.size == 1 else pltpu.HBM) for x in given],
        out_specs=(vmem, vmem),
        scratch_shapes=held
        + [
            pltpu.VMEM((8 + SPAN, W), BF16),
            pltpu.VMEM((Q + Q * T, W), BF16),
            pltpu.VMEM((2, Q * T, C), F32),
            pltpu.VMEM((NZ, ROWS, C), BF16),
            pltpu.VMEM((len(XS), PACK, C), BF16),
            pltpu.VMEM((NX, PACK, C), BF16),
            pltpu.VMEM((NX, Q, C), jnp.int32),
            pltpu.SMEM((NX, Q, C), jnp.int32),
            pltpu.VMEM((pairs, Q, C), F32),
            pltpu.VMEM((T * Q, C), F32),
            pltpu.VMEM((T * Q, C), F32),
            pltpu.VMEM((T * Q, C), F32),
            pltpu.VMEM((T * Q, C), F32),
            pltpu.VMEM((Q, HD, C), F32),
            pltpu.VMEM((Q, HD, C), F32),
            pltpu.VMEM((Q, 4 * T, HD), BF16),
            pltpu.VMEM((Q, T, C), F32),
            pltpu.VMEM((Q, HD, C), F32),
            dma((GIVEN,)), dma((NH - 1,)), dma((NH - 1,)), dma((NH - 1,)), dma((NH - 1,)),
            dma((NZ,)), dma((NZ,)), dma((len(XS),)), dma((len(XS),)), dma((len(XS),)), dma((len(XS),)), dma,
            pltpu.SemaphoreType.REGULAR, pltpu.SemaphoreType.REGULAR,
        ],
        compiler_params=pltpu.CompilerParams(
            collective_id=0, has_side_effects=True, vmem_limit_bytes=32 * 1024 * 1024
        ),
    )(*given)


def solution(mesh):
    in_specs = (
        P("req", None, "head"), P("req", "head"), P("req", "head", None, None), P("req"), P("req"), P("req"), P("req"),
        P("req", "head", None, None), P("req", None, "head"), P("req", "head"), P(None, "head"), P(None, "head"),
        P(None, "head"), P(), P(), P(None, "head"), P("head"), P("head"), P("head"),
    )
    out_specs = (P("req", None, "head"), P("req", "head", None, None))
    return jax.shard_map(per_device, mesh=mesh, in_specs=in_specs, out_specs=out_specs, check_vma=False)
```
